768 devices in a mesh: blk: 96 (over x, y, z_hi), lane: 8 (over z_lo, core).
Axes of the slice: x: 4, y: 8, z: 12 (z_hi: 3, z_lo: 4; z = z_hi * 4 + z_lo), core: 2. Of those that a mesh axis runs over, the one named last changes fastest.
Arguments:
- points: bfloat16 [786432, 128], P(('blk', 'lane')), may hold values from -6 to 6
- probes: bfloat16 [786432, 128], P(('blk', 'lane')), may hold values from -6 to 6
- inv_scale: float32 [128], replicated, may hold values from 0.02 to 0.5
- noise_var: float32 [1], replicated, may hold values from 0.1 to 1
Outputs:
- product: float32 [786432, 128], P(('blk', 'lane'))
The draws below stay inside these ranges and needn't reach their ends.
All inputs are finite; a program needn't handle non-finite values.
Results may differ from the reference program's by a relative error of at most 0.0003.
Values may be sent and summed in bfloat16 or wider, within the bound.
A program may use at most 32 MiB of HBM per device.

```python
import math
import jax
import jax.numpy as jnp
from jax import lax

F = 128
PROBES = 128
POINTS_DEV = 1024
SPAN = 3
POINTS = 786432
N_BLK = 96
N_LANE = 8


def steps_of(stream_key, dims, cuts, smallest, high):
    loudness, own = 1.0, jax.random.fold_in(stream_key, 6)
    for position, parts in cuts:
        steps = jnp.exp(jax.random.uniform(jax.random.fold_in(own, position), (parts,), jnp.float32, smallest / len(cuts), high / len(cuts)))
        loudness = loudness * jnp.repeat(steps, dims[position] // parts).reshape([-1 if axis == position else 1 for axis in range(len(dims))])
    return loudness


def centred(own_key, dims, spread, most, cuts=(), kind=jnp.bfloat16):
    values = jax.random.normal(own_key, dims, jnp.float32) * spread
    if len(cuts) > 0:
        values = steps_of(own_key, dims, cuts, -0.22, 0.18) * values
    return jnp.clip(values, min=-most, max=most).astype(kind)


def setup_inputs(seed: int = 0) -> dict:
    splits = jax.random.split(jax.random.key(seed), 5)
    points = centred(splits[0], (POINTS, F), 1.0, 6.0, ((0, 768),))
    probes = centred(splits[1], (POINTS, PROBES), 1.0, 6.0, ((0, 768),))
    inv_scale = jnp.clip(jnp.exp(jax.random.uniform(splits[2], (F,), jnp.float32, math.log(0.02), math.log(0.5))), 0.02, 0.5)
    noise_var = jnp.clip(jnp.exp(jax.random.uniform(splits[3], (1,), jnp.float32, math.log(0.1), math.log(1.0))), 0.1, 1.0)
    return dict(points=points, probes=probes, inv_scale=inv_scale, noise_var=noise_var)


root_five = 2.23606797749979

def matern_tile(left_rows, right_rows):
    left_sq = lax.optimization_barrier(jnp.sum(left_rows * left_rows, axis=1))
    right_sq = lax.optimization_barrier(jnp.sum(right_rows * right_rows, axis=1))
    cross_term = lax.dot_general(left_rows, right_rows, (((1,), (1,)), ((), ())), precision=lax.Precision.HIGHEST, preferred_element_type=jnp.float32)
    dist_sq = jnp.maximum(left_sq[:, None] + right_sq[None, :] - 2.0 * cross_term, 0.0)
    radius = root_five * jnp.sqrt(dist_sq)
    return (1.0 + radius + 5.0 / 3.0 * dist_sq) * jnp.exp(-radius)

def reference(points, probes, inv_scale, noise_var):
    block_count = N_BLK * N_LANE
    scaled = (points.astype(jnp.float32) * inv_scale[None, :]).reshape(block_count, POINTS_DEV, F)
    probe_rows = probes.astype(jnp.float32).reshape(block_count, POINTS_DEV, PROBES)

    def band_rows(block_index):
        own_rows = scaled[block_index]
        result_sum = noise_var[0] * probe_rows[block_index]
        for block_offset in range(-SPAN, SPAN + 1):
            other_block = ((block_index + block_offset + block_count) % block_count).astype(jnp.int32)
            kernel_tile = matern_tile(own_rows, scaled[other_block])
            result_sum = result_sum + jnp.dot(kernel_tile, probe_rows[other_block], precision=lax.Precision.HIGH, preferred_element_type=jnp.float32)
        return result_sum
    result = lax.map(band_rows, jnp.arange(block_count, dtype=jnp.int32))
    return result.reshape(POINTS, PROBES)
```

```python
import functools
import math

import jax
import jax.numpy as jnp
from jax import lax
from jax.experimental import pallas as pl
from jax.experimental.pallas import tpu as pltpu
from jax.sharding import PartitionSpec as P

MESH = pl.DeviceIdType.MESH
LOG2E = math.log2(math.e)
LN2 = math.log(2.0)
SHIFT = math.log2(LN2 * LN2 / 3.0)
LIN = 3.0 / LN2
CON = 3.0 / (LN2 * LN2)
ROWS = 512
COLS = 256
COMPUTE = True
COMM = True

OWN, PARTNER, LEFT, RIGHT, PLEFT, PRIGHT, FAR = range(7)


def matern(minus_cross, own_sq, other_sq):
    x = jnp.maximum(minus_cross + own_sq + other_sq, 1e-30)
    u = x * lax.rsqrt(x)
    return jnp.exp2(SHIFT - u) * (u * (u + LIN) + CON)


def split(x, parts):
    out = []
    for _ in range(parts):
        piece = x.astype(jnp.bfloat16)
        out.append(piece)
        x = x - piece.astype(jnp.float32)
    return out


def kernel(n_lane, n_dev, p_hbm, v_hbm, scale_ref, noise_ref, o_ref,
           buf, norms, own_sq, left, acc, load_sem, send_sem, recv_sem, nsend_sem, nrecv_sem):
    pts = p_hbm.shape[0]
    n_piece = pts // ROWS
    me = lax.axis_index("blk") * n_lane + lax.axis_index("lane")
    core = lax.rem(me, 2)

    def device(step):
        there = lax.rem(me + step + n_dev, n_dev)
        return (there // n_lane, lax.rem(there, n_lane))

    partner, outer = device(1 - 2 * core), device(2 * core - 1)
    lower, upper = device(-2), device(2)

    loads = [pltpu.make_async_copy(p_hbm, buf.at[OWN, 0], load_sem.at[0]),
             pltpu.make_async_copy(v_hbm, buf.at[OWN, 1], load_sem.at[1])]
    for load in loads:
        load.start()
    if COMM:
        barrier = pltpu.get_barrier_semaphore()
        for there in (partner, outer, lower, upper):
            pl.semaphore_signal(barrier, inc=1, device_id=there, device_id_type=MESH)

    loads[0].wait()
    gain = scale_ref[...] * (math.sqrt(5.0) * LOG2E)
    gain = gain * gain
    ones = jnp.ones((8, 384), jnp.bfloat16)
    for j in range(0, pts, 256):
        p = buf[OWN, 0, j:j + 256, :].astype(jnp.float32)
        hi, lo = split(-2.0 * (p * gain), 2)
        left[j:j + 256, 0:128] = hi
        left[j:j + 256, 128:256] = lo
        q = p * (-0.5 * (hi.astype(jnp.float32) + lo.astype(jnp.float32)))
        row = lax.dot_general(ones, jnp.concatenate(split(q, 3), axis=1), (((1,), (1,)), ((), ())),
                              preferred_element_type=jnp.float32)
        own_sq[:, j:j + 256] = row
        norms[OWN, j // 128:j // 128 + 1, :] = row[0:1, 0:128]
        norms[OWN, j // 128 + 1:j // 128 + 2, :] = row[0:1, 128:256]
    loads[1].wait()

    sent = []

    def send(lane_no, src, dst, piece, there):
        for k in range(2):
            rows = pl.ds(piece * ROWS, ROWS)
            c = pltpu.make_async_remote_copy(
                buf.at[src, k, rows], buf.at[dst, k, rows], send_sem.at[lane_no, piece, k],
                recv_sem.at[dst, piece, k], device_id=there, device_id_type=MESH)
            c.start()
            sent.append(c)

    def send_norm(lane_no, src, dst, there):
        c = pltpu.make_async_remote_copy(
            norms.at[src], norms.at[dst], nsend_sem.at[lane_no], nrecv_sem.at[dst],
            device_id=there, device_id_type=MESH)
        c.start()
        sent.append(c)

    def arrived(slot, piece):
        for k in range(2):
            rows = pl.ds(piece * ROWS, ROWS)
            pltpu.make_async_remote_copy(
                buf.at[slot, k, rows], buf.at[slot, k, rows], send_sem.at[0, 0, 0],
                recv_sem.at[slot, piece, k], device_id=partner, device_id_type=MESH).wait_recv()

    def norm_arrived(slot):
        pltpu.make_async_remote_copy(
            norms.at[slot], norms.at[slot], nsend_sem.at[0],
            nrecv_sem.at[slot], device_id=partner, device_id_type=MESH).wait_recv()

    def compute(slot, piece):
        if not COMPUTE:
            return
        j0 = piece * ROWS
        p = buf[slot, 0, pl.ds(j0, ROWS), :]
        v = buf[slot, 1, pl.ds(j0, ROWS), :]
        pp = jnp.concatenate([p, p], axis=1)
        vt = v.T
        v2 = jnp.concatenate([vt, vt], axis=1)
        cols = []
        for q in range(ROWS // 128):
            row = norms[slot, pl.ds(j0 // 128 + q, 1), :]
            cols.append(jnp.broadcast_to(row, (128, 128)).T)
        other = jnp.concatenate(cols, axis=0)
        other = jnp.concatenate([other] * (COLS // 128), axis=1)
        for i in range(0, pts, COLS):
            c = lax.dot_general(pp, left[i:i + COLS, :], (((1,), (1,)), ((), ())),
                                preferred_element_type=jnp.float32)
            k = matern(c, own_sq[0:1, i:i + COLS], other)
            acc[:, i:i + COLS] += jnp.dot(v2, jnp.concatenate(split(k, 2), axis=0),
                                          preferred_element_type=jnp.float32)

    first, second = 3 - core, 2 + core
    if COMM:
        pl.semaphore_wait(barrier, 4)
        send_norm(0, OWN, RIGHT, lower)
        send_norm(1, OWN, LEFT, upper)
        send_norm(2, OWN, PARTNER, partner)
        for piece in range(n_piece):
            send(0, OWN, RIGHT, piece, lower)
            send(1, OWN, LEFT, piece, upper)
            send(2, OWN, PARTNER, piece, partner)

    acc[...] = jnp.zeros_like(acc)

    def both(slot):
        lax.fori_loop(0, n_piece, lambda piece, c: (compute(slot, piece), c)[1], 0)

    both(OWN)
    if not COMM:
        for slot in range(6):
            both(slot)
    if COMM:
        norm_arrived(PARTNER)
        for piece in range(n_piece):
            arrived(PARTNER, piece)
        both(PARTNER)
        norm_arrived(LEFT)
        norm_arrived(RIGHT)
        send_norm(3, LEFT, PLEFT, partner)
        send_norm(4, RIGHT, PRIGHT, partner)
        send_norm(5, first, FAR, outer)
        for piece in range(n_piece):
            arrived(LEFT, piece)
            send(3, LEFT, PLEFT, piece, partner)
            arrived(RIGHT, piece)
            send(4, RIGHT, PRIGHT, piece, partner)
            send(5, first, FAR, piece, outer)
            lax.fori_loop(LEFT, RIGHT + 1, lambda s, c: (compute(s, piece), c)[1], 0)
            if piece == 0:
                norm_arrived(PLEFT)
                norm_arrived(PRIGHT)
            arrived(PLEFT, piece)
            arrived(PRIGHT, piece)
            lax.fori_loop(PLEFT, PRIGHT + 1, lambda s, c: (compute(s, piece), c)[1], 0)
        norm_arrived(FAR)
        for piece in range(n_piece):
            arrived(FAR, piece)
            compute(FAR, piece)

    noise = noise_ref[0]
    for j in range(0, pts, 256):
        o_ref[j:j + 256, :] = acc[:, j:j + 256].T + noise * buf[OWN, 1, j:j + 256, :].astype(jnp.float32)
    for c in sent:
        c.wait_send()


def body(n_lane, n_dev, points, probes, inv_scale, noise_var):
    pts, feats = points.shape
    n_piece = pts // ROWS
    return pl.pallas_call(
        functools.partial(kernel, n_lane, n_dev),
        out_shape=jax.ShapeDtypeStruct((pts, feats), jnp.float32),
        in_specs=[pl.BlockSpec(memory_space=pl.ANY), pl.BlockSpec(memory_space=pl.ANY),
                  pl.BlockSpec(memory_space=pltpu.VMEM), pl.BlockSpec(memory_space=pltpu.SMEM)],
        out_specs=pl.BlockSpec(memory_space=pltpu.VMEM),
        scratch_shapes=[
            pltpu.VMEM((7, 2, pts, feats), jnp.bfloat16),
            pltpu.VMEM((7, 8, 128), jnp.float32),
            pltpu.VMEM((8, pts), jnp.float32),
            pltpu.VMEM((pts, 2 * feats), jnp.bfloat16),
            pltpu.VMEM((feats, pts), jnp.float32),
            pltpu.SemaphoreType.DMA((2,)),
            pltpu.SemaphoreType.DMA((6, n_piece, 2)),
            pltpu.SemaphoreType.DMA((7, n_piece, 2)),
            pltpu.SemaphoreType.DMA((6,)),
            pltpu.SemaphoreType.DMA((7,)),
        ],
        compiler_params=pltpu.CompilerParams(collective_id=0 if COMM else None, has_side_effects=True),
    )(points, probes, inv_scale.reshape(1, feats), noise_var)


def solution(mesh):
    n_lane = mesh.shape["lane"]
    n_dev = n_lane * mesh.shape["blk"]
    in_specs = (P(("blk", "lane"), None), P(("blk", "lane"), None), P(), P())
    return jax.shard_map(functools.partial(body, n_lane, n_dev), mesh=mesh, in_specs=in_specs,
                         out_specs=P(("blk", "lane"), None), check_vma=False)
```

```python
import functools
import math

import jax
import jax.numpy as jnp
from jax import lax
from jax.experimental import pallas as pl
from jax.experimental.pallas import tpu as pltpu
from jax.sharding import PartitionSpec as P

MESH = pl.DeviceIdType.MESH
LOG2E = math.log2(math.e)
LN2 = math.log(2.0)
SHIFT = math.log2(LN2 * LN2 / 3.0)
LIN = 3.0 / LN2
CON = 3.0 / (LN2 * LN2)
PIECE = 256
ROWS = 512
COLS = 256
RING = 12

OWN, PARTNER, LEFT, RIGHT, PLEFT, PRIGHT, FAR = range(7)
INNER = (((RIGHT, 0), (LEFT, 0), (PRIGHT, 0), (PLEFT, 0), (RIGHT, 1), (LEFT, 1), (PRIGHT, 1), (PLEFT, 1)),
         ((LEFT, 0), (RIGHT, 0), (PLEFT, 0), (PRIGHT, 0), (LEFT, 1), (RIGHT, 1), (PLEFT, 1), (PRIGHT, 1)))
FIRST = ((RIGHT, 0), (PRIGHT, 0), (RIGHT, 1), (PRIGHT, 1), (LEFT, 0), (PLEFT, 0), (LEFT, 1), (PLEFT, 1))


def digits(order, which, base):
    return sum(step[which] * base ** n for n, step in enumerate(order))


def matern(minus_cross, own_sq, other_sq):
    x = jnp.maximum(minus_cross + own_sq + other_sq, 1e-30)
    u = x * lax.rsqrt(x)
    return jnp.exp2(SHIFT - u) * (u * (u + LIN) + CON)


def split(x, parts):
    out = []
    for _ in range(parts):
        piece = x.astype(jnp.bfloat16)
        out.append(piece)
        x = x - piece.astype(jnp.float32)
    return out


def kernel(n_lane, n_dev, p_hbm, v_hbm, scale_ref, o_ref,
           buf, norms, own_sq, left, acc, load_sem, send_sem, recv_sem, nsend_sem, nrecv_sem):
    pts = p_hbm.shape[0]
    n_piece = pts // PIECE
    me = lax.axis_index("blk") * n_lane + lax.axis_index("lane")
    core = lax.rem(me, 2)
    low = 1 - (lax.rem(me // 2, RING) + RING - 1) // RING

    def device(step):
        there = lax.rem(me + step + n_dev, n_dev)
        return (there // n_lane, lax.rem(there, n_lane))

    partner, outer = device(1 - 2 * core), device(2 * core - 1)
    lower, upper = device(-2), device(2)
    inputs = (p_hbm, v_hbm)

    barrier = pltpu.get_barrier_semaphore()
    for there in (partner, outer, lower, upper):
        pl.semaphore_signal(barrier, inc=1, device_id=there, device_id_type=MESH)
    loads = [pltpu.make_async_copy(inputs[k], buf.at[OWN, k], load_sem.at[k]) for k in range(2)]
    for load in loads:
        load.start()

    def copy(flow, src, dst, piece, k, there):
        rows = pl.ds(piece * PIECE, PIECE)
        return pltpu.make_async_remote_copy(
            inputs[k].at[rows] if src is None else buf.at[src, k, rows], buf.at[dst, k, rows],
            send_sem.at[flow, piece, k], recv_sem.at[dst, piece, k],
            device_id=there, device_id_type=MESH)

    def norm_copy(flow, src, dst, there):
        return pltpu.make_async_remote_copy(
            norms.at[src], norms.at[dst], nsend_sem.at[flow], nrecv_sem.at[dst],
            device_id=there, device_id_type=MESH)

    def send(flow, src, dst, piece, there):
        for k in range(2):
            copy(flow, src, dst, piece, k, there).start()

    def arrived(slot, piece):
        for k in range(2):
            copy(0, slot, slot, piece, k, partner).wait_recv()

    pl.semaphore_wait(barrier, 4)
    for piece in range(n_piece):
        send(0, None, RIGHT, piece, lower)
        send(1, None, LEFT, piece, upper)
    for piece in range(n_piece):
        send(2, None, PARTNER, piece, partner)

    loads[0].wait()
    gain = scale_ref[...] * (math.sqrt(5.0) * LOG2E)
    gain = gain * gain
    ones = jnp.ones((8, 384), jnp.bfloat16)
    for j in range(0, pts, 256):
        p = buf[OWN, 0, j:j + 256, :].astype(jnp.float32)
        hi, lo = split(-2.0 * (p * gain), 2)
        left[j:j + 256, 0:128] = hi
        left[j:j + 256, 128:256] = lo
        q = p * (-0.5 * (hi.astype(jnp.float32) + lo.astype(jnp.float32)))
        row = lax.dot_general(ones, jnp.concatenate(split(q, 3), axis=1), (((1,), (1,)), ((), ())),
                              preferred_element_type=jnp.float32)
        own_sq[:, j:j + 256] = row
        norms[OWN, j // 128:j // 128 + 1, :] = row[0:1, 0:128]
        norms[OWN, j // 128 + 1:j // 128 + 2, :] = row[0:1, 128:256]
    loads[1].wait()

    def compute(slot, j0, n_row):
        p = buf[slot, 0, pl.ds(j0, n_row), :]
        v = buf[slot, 1, pl.ds(j0, n_row), :]
        pp = jnp.concatenate([p, p], axis=1)
        vt = v.T
        v2 = jnp.concatenate([vt, vt], axis=1)
        cols = []
        for q in range(n_row // 128):
            row = norms[slot, pl.ds(j0 // 128 + q, 1), :]
            cols.append(jnp.broadcast_to(row, (128, 128)).T)
        other = jnp.concatenate(cols, axis=0)
        other = jnp.concatenate([other] * (COLS // 128), axis=1)
        for i in range(0, pts, COLS):
            c = lax.dot_general(pp, left[i:i + COLS, :], (((1,), (1,)), ((), ())),
                                preferred_element_type=jnp.float32)
            k = matern(c, own_sq[0:1, i:i + COLS], other)
            acc[:, i:i + COLS] += jnp.dot(v2, jnp.concatenate(split(k, 2), axis=0),
                                          preferred_element_type=jnp.float32)

    acc[...] = jnp.zeros_like(acc)

    def near(half, _):
        @pl.when(half == n_half)
        def _():
            norm_copy(0, PARTNER, PARTNER, partner).wait_recv()
            for piece in range(n_piece):
                arrived(PARTNER, piece)

        compute(half // n_half, lax.rem(half, n_half) * ROWS, ROWS)

        @pl.when(half == 0)
        def _():
            norm_copy(0, OWN, RIGHT, lower).start()
            norm_copy(1, OWN, LEFT, upper).start()
            norm_copy(2, OWN, PARTNER, partner).start()
        return 0

    n_half = pts // ROWS
    lax.fori_loop(0, 2 * n_half, near, 0)

    passed_on = 3 - core

    def step(_, codes):
        slots, halves = codes
        slot, half = lax.rem(slots, 8), lax.rem(halves, 2)
        pieces = [half * (ROWS // PIECE) + n for n in range(ROWS // PIECE)]

        @pl.when(half == 0)
        def _():
            norm_copy(0, slot, slot, partner).wait_recv()

            @pl.when(slot < PLEFT)
            def _():
                norm_copy(slot + 1, slot, slot + 2, partner).start()

            @pl.when(slot == passed_on)
            def _():
                norm_copy(5, slot, FAR, outer).start()

        for piece in pieces:
            arrived(slot, piece)

            @pl.when(slot == passed_on)
            def _():
                send(5, slot, FAR, piece, outer)

            @pl.when(slot < PLEFT)
            def _():
                send(slot + 1, slot, slot + 2, piece, partner)

        compute(slot, half * ROWS, ROWS)
        return slots // 8, halves // 2

    slots = low * digits(FIRST, 0, 8) + (1 - low) * (
        (1 - core) * digits(INNER[0], 0, 8) + core * digits(INNER[1], 0, 8))
    halves = low * digits(FIRST, 1, 2) + (1 - low) * digits(INNER[0], 1, 2)
    lax.fori_loop(0, len(FIRST), step, (slots, halves))

    norm_copy(0, FAR, FAR, partner).wait_recv()

    def last(piece, _):
        arrived(FAR, piece)
        compute(FAR, piece * PIECE, PIECE)
        return 0

    lax.fori_loop(0, n_piece, last, 0)

    for j in range(0, pts, 256):
        o_ref[j:j + 256, :] = acc[:, j:j + 256].T
    for flow in range(6):
        norm_copy(flow, OWN, PARTNER, partner).wait_send()
        for piece in range(n_piece):
            for k in range(2):
                copy(flow, OWN, PARTNER, piece, k, partner).wait_send()


def body(n_lane, n_dev, points, probes, inv_scale, noise_var):
    pts, feats = points.shape
    n_piece = pts // PIECE
    product = pl.pallas_call(
        functools.partial(kernel, n_lane, n_dev),
        out_shape=jax.ShapeDtypeStruct((pts, feats), jnp.float32),
        in_specs=[pl.BlockSpec(memory_space=pl.ANY), pl.BlockSpec(memory_space=pl.ANY),
                  pl.BlockSpec(memory_space=pltpu.VMEM)],
        out_specs=pl.BlockSpec(memory_space=pltpu.VMEM),
        scratch_shapes=[
            pltpu.VMEM((7, 2, pts, feats), jnp.bfloat16),
            pltpu.VMEM((7, 8, 128), jnp.float32),
            pltpu.VMEM((8, pts), jnp.float32),
            pltpu.VMEM((pts, 2 * feats), jnp.bfloat16),
            pltpu.VMEM((feats, pts), jnp.float32),
            pltpu.SemaphoreType.DMA((2,)),
            pltpu.SemaphoreType.DMA((6, n_piece, 2)),
            pltpu.SemaphoreType.DMA((7, n_piece, 2)),
            pltpu.SemaphoreType.DMA((6,)),
            pltpu.SemaphoreType.DMA((7,)),
        ],
        compiler_params=pltpu.CompilerParams(collective_id=0, has_side_effects=True),
    )(points, probes, inv_scale.reshape(1, feats))
    return product + noise_var[0] * probes.astype(jnp.float32)


def solution(mesh):
    n_lane = mesh.shape["lane"]
    n_dev = n_lane * mesh.shape["blk"]
    in_specs = (P(("blk", "lane"), None), P(("blk", "lane"), None), P(), P())
    return jax.shard_map(functools.partial(body, n_lane, n_dev), mesh=mesh, in_specs=in_specs,
                         out_specs=P(("blk", "lane"), None), check_vma=False)
```

```python
import functools
import math

import jax
import jax.numpy as jnp
from jax import lax
from jax.experimental import pallas as pl
from jax.experimental.pallas import tpu as pltpu
from jax.sharding import PartitionSpec as P

MESH = pl.DeviceIdType.MESH
LOG2E = math.log2(math.e)
LN2 = math.log(2.0)
SHIFT = math.log2(LN2 * LN2 / 3.0)
LIN = 3.0 / LN2
CON = 3.0 / (LN2 * LN2)
PIECE = 256
ROWS = 512
COLS = 256
RING = 12

OWN, PARTNER, LEFT, RIGHT, PLEFT, PRIGHT, FAR = range(7)
INNER = (((RIGHT, 0), (LEFT, 0), (PRIGHT, 0), (PLEFT, 0), (RIGHT, 1), (LEFT, 1), (PRIGHT, 1), (PLEFT, 1)),
         ((LEFT, 0), (RIGHT, 0), (PLEFT, 0), (PRIGHT, 0), (LEFT, 1), (RIGHT, 1), (PLEFT, 1), (PRIGHT, 1)))
FIRST = ((RIGHT, 0), (PRIGHT, 0), (RIGHT, 1), (PRIGHT, 1), (LEFT, 0), (PLEFT, 0), (LEFT, 1), (PLEFT, 1))


def digits(order, which, base):
    return sum(step[which] * base ** n for n, step in enumerate(order))


def matern(minus_cross, own_sq, other_sq):
    x = jnp.maximum(minus_cross + own_sq + other_sq, 1e-30)
    u = x * lax.rsqrt(x)
    return jnp.exp2(SHIFT - u) * (u * (u + LIN) + CON)


def split(x, parts):
    out = []
    for _ in range(parts):
        piece = x.astype(jnp.bfloat16)
        out.append(piece)
        x = x - piece.astype(jnp.float32)
    return out


def kernel(n_lane, n_dev, p_hbm, v_hbm, scale_ref, o_ref,
           buf, norms, own_sq, left, acc, load_sem, send_sem, recv_sem, nsend_sem, nrecv_sem):
    pts = p_hbm.shape[0]
    n_piece = pts // PIECE
    me = lax.axis_index("blk") * n_lane + lax.axis_index("lane")
    core = lax.rem(me, 2)
    low = 1 - (lax.rem(me // 2, RING) + RING - 1) // RING

    def device(step):
        there = lax.rem(me + step + n_dev, n_dev)
        return (there // n_lane, lax.rem(there, n_lane))

    partner, outer = device(1 - 2 * core), device(2 * core - 1)
    lower, upper = device(-2), device(2)
    inputs = (p_hbm, v_hbm)

    barrier = pltpu.get_barrier_semaphore()
    for there in (partner, outer, lower, upper):
        pl.semaphore_signal(barrier, inc=1, device_id=there, device_id_type=MESH)
    loads = [pltpu.make_async_copy(inputs[k], buf.at[OWN, k], load_sem.at[k]) for k in range(2)]
    for load in loads:
        load.start()

    def copy(flow, src, dst, piece, there):
        rows = pl.ds(piece * PIECE, PIECE)
        return pltpu.make_async_remote_copy(
            buf.at[src, :, rows], buf.at[dst, :, rows], send_sem.at[flow, piece], recv_sem.at[dst, piece],
            device_id=there, device_id_type=MESH)

    def norm_copy(flow, src, dst, there):
        return pltpu.make_async_remote_copy(
            norms.at[src], norms.at[dst], nsend_sem.at[flow], nrecv_sem.at[dst],
            device_id=there, device_id_type=MESH)

    def send_own(piece):
        copy(0, OWN, RIGHT, piece, lower).start()
        copy(1, OWN, LEFT, piece, upper).start()
        copy(2, OWN, PARTNER, piece, partner).start()

    def arrived(slot, piece):
        copy(0, slot, slot, piece, partner).wait_recv()

    for load in loads:
        load.wait()
    pl.semaphore_wait(barrier, 4)
    send_own(0)

    gain = scale_ref[...] * (math.sqrt(5.0) * LOG2E)
    gain = gain * gain
    ones = jnp.ones((8, 384), jnp.bfloat16)
    for j in range(0, pts, 256):
        p = buf[OWN, 0, j:j + 256, :].astype(jnp.float32)
        hi, lo = split(-2.0 * (p * gain), 2)
        left[j:j + 256, 0:128] = hi
        left[j:j + 256, 128:256] = lo
        q = p * (-0.5 * (hi.astype(jnp.float32) + lo.astype(jnp.float32)))
        row = lax.dot_general(ones, jnp.concatenate(split(q, 3), axis=1), (((1,), (1,)), ((), ())),
                              preferred_element_type=jnp.float32)
        own_sq[:, j:j + 256] = row
        norms[OWN, j // 128:j // 128 + 1, :] = row[0:1, 0:128]
        norms[OWN, j // 128 + 1:j // 128 + 2, :] = row[0:1, 128:256]
    acc[...] = jnp.zeros_like(acc)
    norm_copy(0, OWN, RIGHT, lower).start()
    norm_copy(1, OWN, LEFT, upper).start()
    norm_copy(2, OWN, PARTNER, partner).start()
    for piece in range(1, n_piece):
        send_own(piece)

    def compute(slot, j0, n_row):
        p = buf[slot, 0, pl.ds(j0, n_row), :]
        v = buf[slot, 1, pl.ds(j0, n_row), :]
        pp = jnp.concatenate([p, p], axis=1)
        vt = v.T
        v2 = jnp.concatenate([vt, vt], axis=1)
        cols = []
        for q in range(n_row // 128):
            row = norms[slot, pl.ds(j0 // 128 + q, 1), :]
            cols.append(jnp.broadcast_to(row, (128, 128)).T)
        other = jnp.concatenate(cols, axis=0)
        other = jnp.concatenate([other] * (COLS // 128), axis=1)
        for i in range(0, pts, COLS):
            c = lax.dot_general(pp, left[i:i + COLS, :], (((1,), (1,)), ((), ())),
                                preferred_element_type=jnp.float32)
            k = matern(c, own_sq[0:1, i:i + COLS], other)
            acc[:, i:i + COLS] += jnp.dot(v2, jnp.concatenate(split(k, 2), axis=0),
                                          preferred_element_type=jnp.float32)

    def near(half, _):
        @pl.when(half == n_half)
        def _():
            norm_copy(0, PARTNER, PARTNER, partner).wait_recv()
            for piece in range(n_piece):
                arrived(PARTNER, piece)

        compute(half // n_half, lax.rem(half, n_half) * ROWS, ROWS)
        return 0

    n_half = pts // ROWS
    lax.fori_loop(0, 2 * n_half, near, 0)

    passed_on = 3 - core

    def step(n, codes):
        slots, halves = codes
        slot, half = lax.rem(slots, 8), lax.rem(halves, 2)

        for near_slot in (LEFT, RIGHT):
            for piece in range(n_piece):
                when_low = 4 * (near_slot == LEFT) + 2 * (piece // 2)
                when = low * when_low + (1 - low) * (0, 0, 1, 2)[piece]

                @pl.when(n == when)
                def _():
                    if piece == 0:
                        norm_copy(0, near_slot, near_slot, partner).wait_recv()
                        norm_copy(near_slot + 1, near_slot, near_slot + 2, partner).start()
                    arrived(near_slot, piece)

                    @pl.when(near_slot == passed_on)
                    def _():
                        if piece == 0:
                            norm_copy(5, near_slot, FAR, outer).start()
                        copy(5, near_slot, FAR, piece, outer).start()

                    copy(near_slot + 1, near_slot, near_slot + 2, piece, partner).start()

        @pl.when(slot >= PLEFT)
        def _():
            @pl.when(half == 0)
            def _():
                norm_copy(0, slot, slot, partner).wait_recv()

            for n_th in range(ROWS // PIECE):
                arrived(slot, half * (ROWS // PIECE) + n_th)

        compute(slot, half * ROWS, ROWS)
        return slots // 8, halves // 2

    slots = low * digits(FIRST, 0, 8) + (1 - low) * (
        (1 - core) * digits(INNER[0], 0, 8) + core * digits(INNER[1], 0, 8))
    halves = low * digits(FIRST, 1, 2) + (1 - low) * digits(INNER[0], 1, 2)
    lax.fori_loop(0, len(FIRST), step, (slots, halves))

    norm_copy(0, FAR, FAR, partner).wait_recv()

    def last(piece, _):
        arrived(FAR, piece)
        compute(FAR, piece * PIECE, PIECE)
        return 0

    lax.fori_loop(0, n_piece, last, 0)

    for j in range(0, pts, 256):
        o_ref[j:j + 256, :] = acc[:, j:j + 256].T
    for flow in range(6):
        norm_copy(flow, OWN, PARTNER, partner).wait_send()
        for piece in range(n_piece):
            copy(flow, OWN, PARTNER, piece, partner).wait_send()


def body(n_lane, n_dev, points, probes, inv_scale, noise_var):
    pts, feats = points.shape
    n_piece = pts // PIECE
    product = pl.pallas_call(
        functools.partial(kernel, n_lane, n_dev),
        out_shape=jax.ShapeDtypeStruct((pts, feats), jnp.float32),
        in_specs=[pl.BlockSpec(memory_space=pl.ANY), pl.BlockSpec(memory_space=pl.ANY),
                  pl.BlockSpec(memory_space=pltpu.VMEM)],
        out_specs=pl.BlockSpec(memory_space=pltpu.VMEM),
        scratch_shapes=[
            pltpu.VMEM((7, 2, pts, feats), jnp.bfloat16),
            pltpu.VMEM((7, 8, 128), jnp.float32),
            pltpu.VMEM((8, pts), jnp.float32),
            pltpu.VMEM((pts, 2 * feats), jnp.bfloat16),
            pltpu.VMEM((feats, pts), jnp.float32),
            pltpu.SemaphoreType.DMA((2,)),
            pltpu.SemaphoreType.DMA((6, n_piece)),
            pltpu.SemaphoreType.DMA((7, n_piece)),
            pltpu.SemaphoreType.DMA((6,)),
            pltpu.SemaphoreType.DMA((7,)),
        ],
        compiler_params=pltpu.CompilerParams(collective_id=0, has_side_effects=True),
    )(points, probes, inv_scale.reshape(1, feats))
    return product + noise_var[0] * probes.astype(jnp.float32)


def solution(mesh):
    n_lane = mesh.shape["lane"]
    n_dev = n_lane * mesh.shape["blk"]
    in_specs = (P(("blk", "lane"), None), P(("blk", "lane"), None), P(), P())
    return jax.shard_map(functools.partial(body, n_lane, n_dev), mesh=mesh, in_specs=in_specs,
                         out_specs=P(("blk", "lane"), None), check_vma=False)
```

```python
import functools
import math

import jax
import jax.numpy as jnp
from jax import lax
from jax.experimental import pallas as pl
from jax.experimental.pallas import tpu as pltpu
from jax.sharding import PartitionSpec as P

MESH = pl.DeviceIdType.MESH
LOG2E = math.log2(math.e)
LN2 = math.log(2.0)
SHIFT = math.log2(LN2 * LN2 / 3.0)
LIN = 3.0 / LN2
CON = 3.0 / (LN2 * LN2)
PIECE = 256
ROWS = 512
COLS = 256
RING = 12

OWN, PARTNER, LEFT, RIGHT, PLEFT, PRIGHT, FAR = range(7)
INNER = (((RIGHT, 0), (LEFT, 0), (PRIGHT, 0), (PLEFT, 0), (RIGHT, 1), (LEFT, 1), (PRIGHT, 1), (PLEFT, 1)),
         ((LEFT, 0), (RIGHT, 0), (PLEFT, 0), (PRIGHT, 0), (LEFT, 1), (RIGHT, 1), (PLEFT, 1), (PRIGHT, 1)))
FIRST = ((RIGHT, 0), (PRIGHT, 0), (RIGHT, 1), (PRIGHT, 1), (LEFT, 0), (PLEFT, 0), (LEFT, 1), (PLEFT, 1))


def digits(order, which, base):
    return sum(step[which] * base ** n for n, step in enumerate(order))


def matern(minus_cross, own_sq, other_sq):
    x = jnp.maximum(minus_cross + own_sq + other_sq, 1e-30)
    u = x * lax.rsqrt(x)
    return jnp.exp2(SHIFT - u) * (u * (u + LIN) + CON)


def split(x, parts):
    out = []
    for _ in range(parts):
        piece = x.astype(jnp.bfloat16)
        out.append(piece)
        x = x - piece.astype(jnp.float32)
    return out


def kernel(n_lane, n_dev, p_hbm, v_hbm, scale_ref, o_ref,
           buf, norms, own_sq, left, acc, load_sem, send_sem, recv_sem, nsend_sem, nrecv_sem):
    pts = p_hbm.shape[0]
    n_piece = pts // PIECE
    me = lax.axis_index("blk") * n_lane + lax.axis_index("lane")
    core = lax.rem(me, 2)
    low = 1 - (lax.rem(me // 2, RING) + RING - 2) // RING

    def device(step):
        there = lax.rem(me + step + n_dev, n_dev)
        return (there // n_lane, lax.rem(there, n_lane))

    partner, outer = device(1 - 2 * core), device(2 * core - 1)
    lower, upper = device(-2), device(2)
    inputs = (p_hbm, v_hbm)

    barrier = pltpu.get_barrier_semaphore()
    for there in (partner, outer, lower, upper):
        pl.semaphore_signal(barrier, inc=1, device_id=there, device_id_type=MESH)
    loads = [pltpu.make_async_copy(inputs[k], buf.at[OWN, k], load_sem.at[k]) for k in range(2)]
    for load in loads:
        load.start()

    def copy(flow, src, dst, piece, there):
        rows = pl.ds(piece * PIECE, PIECE)
        return pltpu.make_async_remote_copy(
            buf.at[src, :, rows], buf.at[dst, :, rows], send_sem.at[flow, piece], recv_sem.at[dst, piece],
            device_id=there, device_id_type=MESH)

    def norm_copy(flow, src, dst, there):
        return pltpu.make_async_remote_copy(
            norms.at[src], norms.at[dst], nsend_sem.at[flow], nrecv_sem.at[dst],
            device_id=there, device_id_type=MESH)

    def send_own(piece):
        copy(0, OWN, RIGHT, piece, lower).start()
        copy(1, OWN, LEFT, piece, upper).start()
        copy(2, OWN, PARTNER, piece, partner).start()

    def arrived(slot, piece):
        copy(0, slot, slot, piece, partner).wait_recv()

    for load in loads:
        load.wait()
    pl.semaphore_wait(barrier, 4)
    send_own(0)

    gain = scale_ref[...] * (math.sqrt(5.0) * LOG2E)
    gain = gain * gain
    ones = jnp.ones((8, 384), jnp.bfloat16)
    for j in range(0, pts, 256):
        p = buf[OWN, 0, j:j + 256, :].astype(jnp.float32)
        hi, lo = split(-2.0 * (p * gain), 2)
        left[j:j + 256, 0:128] = hi
        left[j:j + 256, 128:256] = lo
        q = p * (-0.5 * (hi.astype(jnp.float32) + lo.astype(jnp.float32)))
        row = lax.dot_general(ones, jnp.concatenate(split(q, 3), axis=1), (((1,), (1,)), ((), ())),
                              preferred_element_type=jnp.float32)
        own_sq[:, j:j + 256] = row
        norms[OWN, j // 128:j // 128 + 1, :] = row[0:1, 0:128]
        norms[OWN, j // 128 + 1:j // 128 + 2, :] = row[0:1, 128:256]
    acc[...] = jnp.zeros_like(acc)
    norm_copy(0, OWN, RIGHT, lower).start()
    norm_copy(1, OWN, LEFT, upper).start()
    norm_copy(2, OWN, PARTNER, partner).start()
    for piece in range(1, n_piece):
        send_own(piece)

    def compute(slot, j0, n_row):
        p = buf[slot, 0, pl.ds(j0, n_row), :]
        v = buf[slot, 1, pl.ds(j0, n_row), :]
        pp = jnp.concatenate([p, p], axis=1)
        vt = v.T
        v2 = jnp.concatenate([vt, vt], axis=1)
        cols = []
        for q in range(n_row // 128):
            row = norms[slot, pl.ds(j0 // 128 + q, 1), :]
            cols.append(jnp.broadcast_to(row, (128, 128)).T)
        other = jnp.concatenate(cols, axis=0)
        other = jnp.concatenate([other] * (COLS // 128), axis=1)
        for i in range(0, pts, COLS):
            c = lax.dot_general(pp, left[i:i + COLS, :], (((1,), (1,)), ((), ())),
                                preferred_element_type=jnp.float32)
            k = matern(c, own_sq[0:1, i:i + COLS], other)
            acc[:, i:i + COLS] += jnp.dot(v2, jnp.concatenate(split(k, 2), axis=0),
                                          preferred_element_type=jnp.float32)

    def near(half, _):
        @pl.when(half == n_half)
        def _():
            norm_copy(0, PARTNER, PARTNER, partner).wait_recv()
            for piece in range(n_piece):
                arrived(PARTNER, piece)

        compute(half // n_half, lax.rem(half, n_half) * ROWS, ROWS)
        return 0

    n_half = pts // ROWS
    lax.fori_loop(0, 2 * n_half, near, 0)

    passed_on = 3 - core

    def step(n, codes):
        slots, halves = codes
        slot, half = lax.rem(slots, 8), lax.rem(halves, 2)

        for near_slot in (LEFT, RIGHT):
            for piece in range(n_piece):
                when_low = 4 * (near_slot == LEFT) + 2 * (piece // 2)
                when = low * when_low + (1 - low) * (0, 0, 1, 2)[piece]

                @pl.when(n == when)
                def _():
                    if piece == 0:
                        norm_copy(0, near_slot, near_slot, partner).wait_recv()
                        norm_copy(near_slot + 1, near_slot, near_slot + 2, partner).start()
                    arrived(near_slot, piece)

                    @pl.when(near_slot == passed_on)
                    def _():
                        if piece == 0:
                            norm_copy(5, near_slot, FAR, outer).start()
                        copy(5, near_slot, FAR, piece, outer).start()

                    copy(near_slot + 1, near_slot, near_slot + 2, piece, partner).start()

        @pl.when(slot >= PLEFT)
        def _():
            @pl.when(half == 0)
            def _():
                norm_copy(0, slot, slot, partner).wait_recv()

            for n_th in range(ROWS // PIECE):
                arrived(slot, half * (ROWS // PIECE) + n_th)

        compute(slot, half * ROWS, ROWS)
        return slots // 8, halves // 2

    slots = low * digits(FIRST, 0, 8) + (1 - low) * (
        (1 - core) * digits(INNER[0], 0, 8) + core * digits(INNER[1], 0, 8))
    halves = low * digits(FIRST, 1, 2) + (1 - low) * digits(INNER[0], 1, 2)
    lax.fori_loop(0, len(FIRST), step, (slots, halves))

    norm_copy(0, FAR, FAR, partner).wait_recv()

    def last(piece, _):
        arrived(FAR, piece)
        compute(FAR, piece * PIECE, PIECE)
        return 0

    lax.fori_loop(0, n_piece, last, 0)

    for j in range(0, pts, 256):
        o_ref[j:j + 256, :] = acc[:, j:j + 256].T
    for flow in range(6):
        norm_copy(flow, OWN, PARTNER, partner).wait_send()
        for piece in range(n_piece):
            copy(flow, OWN, PARTNER, piece, partner).wait_send()


def body(n_lane, n_dev, points, probes, inv_scale, noise_var):
    pts, feats = points.shape
    n_piece = pts // PIECE
    product = pl.pallas_call(
        functools.partial(kernel, n_lane, n_dev),
        out_shape=jax.ShapeDtypeStruct((pts, feats), jnp.float32),
        in_specs=[pl.BlockSpec(memory_space=pl.ANY), pl.BlockSpec(memory_space=pl.ANY),
                  pl.BlockSpec(memory_space=pltpu.VMEM)],
        out_specs=pl.BlockSpec(memory_space=pltpu.VMEM),
        scratch_shapes=[
            pltpu.VMEM((7, 2, pts, feats), jnp.bfloat16),
            pltpu.VMEM((7, 8, 128), jnp.float32),
            pltpu.VMEM((8, pts), jnp.float32),
            pltpu.VMEM((pts, 2 * feats), jnp.bfloat16),
            pltpu.VMEM((feats, pts), jnp.float32),
            pltpu.SemaphoreType.DMA((2,)),
            pltpu.SemaphoreType.DMA((6, n_piece)),
            pltpu.SemaphoreType.DMA((7, n_piece)),
            pltpu.SemaphoreType.DMA((6,)),
            pltpu.SemaphoreType.DMA((7,)),
        ],
        compiler_params=pltpu.CompilerParams(collective_id=0, has_side_effects=True),
    )(points, probes, inv_scale.reshape(1, feats))
    return product + noise_var[0] * probes.astype(jnp.float32)


def solution(mesh):
    n_lane = mesh.shape["lane"]
    n_dev = n_lane * mesh.shape["blk"]
    in_specs = (P(("blk", "lane"), None), P(("blk", "lane"), None), P(), P())
    return jax.shard_map(functools.partial(body, n_lane, n_dev), mesh=mesh, in_specs=in_specs,
                         out_specs=P(("blk", "lane"), None), check_vma=False)
```

```python
import functools
import math

import jax
import jax.numpy as jnp
from jax import lax
from jax.experimental import pallas as pl
from jax.experimental.pallas import tpu as pltpu
from jax.sharding import PartitionSpec as P

MESH = pl.DeviceIdType.MESH
LOG2E = math.log2(math.e)
LN2 = math.log(2.0)
SHIFT = math.log2(LN2 * LN2 / 3.0)
LIN = 3.0 / LN2
CON = 3.0 / (LN2 * LN2)
PIECE = 256
ROWS = 512
COLS = 256
RING = 12

OWN, PARTNER, LEFT, RIGHT, PLEFT, PRIGHT, FAR = range(7)
INNER = (((RIGHT, 0), (LEFT, 0), (PRIGHT, 0), (PLEFT, 0), (RIGHT, 1), (LEFT, 1), (PRIGHT, 1), (PLEFT, 1)),
         ((LEFT, 0), (RIGHT, 0), (PLEFT, 0), (PRIGHT, 0), (LEFT, 1), (RIGHT, 1), (PLEFT, 1), (PRIGHT, 1)))
FIRST = ((RIGHT, 0), (PRIGHT, 0), (RIGHT, 1), (PRIGHT, 1), (LEFT, 0), (PLEFT, 0), (LEFT, 1), (PLEFT, 1))


def digits(order, which, base):
    return sum(step[which] * base ** n for n, step in enumerate(order))


def matern(minus_cross, own_sq, other_sq):
    x = jnp.maximum(minus_cross + own_sq + other_sq, 1e-30)
    u = x * lax.rsqrt(x)
    return jnp.exp2(SHIFT - u) * (u * (u + LIN) + CON)


def split(x, parts):
    out = []
    for _ in range(parts):
        piece = x.astype(jnp.bfloat16)
        out.append(piece)
        x = x - piece.astype(jnp.float32)
    return out


def kernel(n_lane, n_dev, p_hbm, v_hbm, scale_ref, o_ref,
           buf, norms, own_sq, left, acc, load_sem, send_sem, recv_sem, nsend_sem, nrecv_sem):
    pts = p_hbm.shape[0]
    n_piece = pts // PIECE
    me = lax.axis_index("blk") * n_lane + lax.axis_index("lane")
    core = lax.rem(me, 2)
    low = 1 - (lax.rem(me // 2, RING) + RING - 2) // RING

    def device(step):
        there = lax.rem(me + step + n_dev, n_dev)
        return (there // n_lane, lax.rem(there, n_lane))

    partner, outer = device(1 - 2 * core), device(2 * core - 1)
    lower, upper = device(-2), device(2)
    inputs = (p_hbm, v_hbm)

    barrier = pltpu.get_barrier_semaphore()
    for there in (partner, outer, lower, upper):
        pl.semaphore_signal(barrier, inc=1, device_id=there, device_id_type=MESH)
    loads = [pltpu.make_async_copy(inputs[k], buf.at[OWN, k], load_sem.at[k]) for k in range(2)]
    for load in loads:
        load.start()

    def copy(flow, src, dst, piece, there):
        rows = pl.ds(piece * PIECE, PIECE)
        return pltpu.make_async_remote_copy(
            buf.at[src, :, rows], buf.at[dst, :, rows], send_sem.at[flow, piece], recv_sem.at[dst, piece],
            device_id=there, device_id_type=MESH)

    def norm_copy(flow, src, dst, there):
        return pltpu.make_async_remote_copy(
            norms.at[src], norms.at[dst], nsend_sem.at[flow], nrecv_sem.at[dst],
            device_id=there, device_id_type=MESH)

    def send_own(piece):
        copy(0, OWN, RIGHT, piece, lower).start()
        copy(1, OWN, LEFT, piece, upper).start()
        copy(2, OWN, PARTNER, piece, partner).start()

    def arrived(slot, piece):
        copy(0, slot, slot, piece, partner).wait_recv()

    for load in loads:
        load.wait()
    pl.semaphore_wait(barrier, 4)
    send_own(0)

    gain = scale_ref[...] * (math.sqrt(5.0) * LOG2E)
    gain = gain * gain
    ones = jnp.ones((8, 384), jnp.bfloat16)
    for j in range(0, pts, 256):
        p = buf[OWN, 0, j:j + 256, :].astype(jnp.float32)
        hi, lo = split(-2.0 * (p * gain), 2)
        left[j:j + 256, 0:128] = hi
        left[j:j + 256, 128:256] = lo
        q = p * (-0.5 * (hi.astype(jnp.float32) + lo.astype(jnp.float32)))
        row = lax.dot_general(ones, jnp.concatenate(split(q, 3), axis=1), (((1,), (1,)), ((), ())),
                              preferred_element_type=jnp.float32)
        own_sq[:, j:j + 256] = row
        norms[OWN, j // 128:j // 128 + 1, :] = row[0:1, 0:128]
        norms[OWN, j // 128 + 1:j // 128 + 2, :] = row[0:1, 128:256]
    acc[...] = jnp.zeros_like(acc)
    norm_copy(0, OWN, RIGHT, lower).start()
    norm_copy(1, OWN, LEFT, upper).start()
    norm_copy(2, OWN, PARTNER, partner).start()
    for piece in range(1, n_piece):
        send_own(piece)

    def compute(slot, j0, n_row):
        p = buf[slot, 0, pl.ds(j0, n_row), :]
        v = buf[slot, 1, pl.ds(j0, n_row), :]
        pp = jnp.concatenate([p, p], axis=1)
        vt = v.T
        v2 = jnp.concatenate([vt, vt], axis=1)
        cols = []
        for q in range(n_row // 128):
            row = norms[slot, pl.ds(j0 // 128 + q, 1), :]
            cols.append(jnp.broadcast_to(row, (128, 128)).T)
        other = jnp.concatenate(cols, axis=0)
        other = jnp.concatenate([other] * (COLS // 128), axis=1)
        for i in range(0, pts, COLS):
            c = lax.dot_general(pp, left[i:i + COLS, :], (((1,), (1,)), ((), ())),
                                preferred_element_type=jnp.float32)
            k = matern(c, own_sq[0:1, i:i + COLS], other)
            acc[:, i:i + COLS] += jnp.dot(v2, jnp.concatenate(split(k, 2), axis=0),
                                          preferred_element_type=jnp.float32)

    def near(half, _):
        @pl.when(half == n_half)
        def _():
            norm_copy(0, PARTNER, PARTNER, partner).wait_recv()
            for piece in range(n_piece):
                arrived(PARTNER, piece)

        compute(half // n_half, lax.rem(half, n_half) * ROWS, ROWS)
        return 0

    n_half = pts // ROWS
    lax.fori_loop(0, 2 * n_half, near, 0)

    passed_on = 3 - core
    early = low * core

    def far(n_row):
        norm_copy(0, FAR, FAR, partner).wait_recv()

        def part(n, _):
            for n_th in range(n_row // PIECE):
                arrived(FAR, n * (n_row // PIECE) + n_th)
            compute(FAR, n * n_row, n_row)
            return 0

        lax.fori_loop(0, pts // n_row, part, 0)

    def step(n, codes):
        slots, halves = codes
        slot, half = lax.rem(slots, 8), lax.rem(halves, 2)

        @pl.when(n == 4 + 8 * (1 - early))
        def _():
            far(ROWS)

        for near_slot in (LEFT, RIGHT):
            for piece in range(n_piece):
                when_low = 4 * (near_slot == LEFT) + 2 * (piece // 2)
                when = low * when_low + (1 - low) * (0, 0, 1, 2)[piece]

                @pl.when(n == when)
                def _():
                    if piece == 0:
                        norm_copy(0, near_slot, near_slot, partner).wait_recv()
                        norm_copy(near_slot + 1, near_slot, near_slot + 2, partner).start()
                    arrived(near_slot, piece)

                    @pl.when(near_slot == passed_on)
                    def _():
                        if piece == 0:
                            norm_copy(5, near_slot, FAR, outer).start()
                        copy(5, near_slot, FAR, piece, outer).start()

                    copy(near_slot + 1, near_slot, near_slot + 2, piece, partner).start()

        @pl.when(slot >= PLEFT)
        def _():
            @pl.when(half == 0)
            def _():
                norm_copy(0, slot, slot, partner).wait_recv()

            for n_th in range(ROWS // PIECE):
                arrived(slot, half * (ROWS // PIECE) + n_th)

        compute(slot, half * ROWS, ROWS)
        return slots // 8, halves // 2

    slots = low * digits(FIRST, 0, 8) + (1 - low) * (
        (1 - core) * digits(INNER[0], 0, 8) + core * digits(INNER[1], 0, 8))
    halves = low * digits(FIRST, 1, 2) + (1 - low) * digits(INNER[0], 1, 2)
    lax.fori_loop(0, len(FIRST), step, (slots, halves))

    @pl.when(early == 0)
    def _():
        far(PIECE)

    for j in range(0, pts, 256):
        o_ref[j:j + 256, :] = acc[:, j:j + 256].T
    for flow in range(6):
        norm_copy(flow, OWN, PARTNER, partner).wait_send()
        for piece in range(n_piece):
            copy(flow, OWN, PARTNER, piece, partner).wait_send()


def body(n_lane, n_dev, points, probes, inv_scale, noise_var):
    pts, feats = points.shape
    n_piece = pts // PIECE
    product = pl.pallas_call(
        functools.partial(kernel, n_lane, n_dev),
        out_shape=jax.ShapeDtypeStruct((pts, feats), jnp.float32),
        in_specs=[pl.BlockSpec(memory_space=pl.ANY), pl.BlockSpec(memory_space=pl.ANY),
                  pl.BlockSpec(memory_space=pltpu.VMEM)],
        out_specs=pl.BlockSpec(memory_space=pltpu.VMEM),
        scratch_shapes=[
            pltpu.VMEM((7, 2, pts, feats), jnp.bfloat16),
            pltpu.VMEM((7, 8, 128), jnp.float32),
            pltpu.VMEM((8, pts), jnp.float32),
            pltpu.VMEM((pts, 2 * feats), jnp.bfloat16),
            pltpu.VMEM((feats, pts), jnp.float32),
            pltpu.SemaphoreType.DMA((2,)),
            pltpu.SemaphoreType.DMA((6, n_piece)),
            pltpu.SemaphoreType.DMA((7, n_piece)),
            pltpu.SemaphoreType.DMA((6,)),
            pltpu.SemaphoreType.DMA((7,)),
        ],
        compiler_params=pltpu.CompilerParams(collective_id=0, has_side_effects=True),
    )(points, probes, inv_scale.reshape(1, feats))
    return product + noise_var[0] * probes.astype(jnp.float32)


def solution(mesh):
    n_lane = mesh.shape["lane"]
    n_dev = n_lane * mesh.shape["blk"]
    in_specs = (P(("blk", "lane"), None), P(("blk", "lane"), None), P(), P())
    return jax.shard_map(functools.partial(body, n_lane, n_dev), mesh=mesh, in_specs=in_specs,
                         out_specs=P(("blk", "lane"), None), check_vma=False)
```

```python
import functools
import math

import jax
import jax.numpy as jnp
from jax import lax
from jax.experimental import pallas as pl
from jax.experimental.pallas import tpu as pltpu
from jax.sharding import PartitionSpec as P

MESH = pl.DeviceIdType.MESH
LOG2E = math.log2(math.e)
LN2 = math.log(2.0)
SHIFT = math.log2(LN2 * LN2 / 3.0)
LIN = 3.0 / LN2
CON = 3.0 / (LN2 * LN2)
PIECE = 256
ROWS = 512
COLS = 256
RING = 12

OWN, PARTNER, LEFT, RIGHT, PLEFT, PRIGHT, FAR = range(7)
INNER = (((RIGHT, 0), (LEFT, 0), (PRIGHT, 0), (PLEFT, 0), (RIGHT, 1), (LEFT, 1), (PRIGHT, 1), (PLEFT, 1)),
         ((LEFT, 0), (RIGHT, 0), (PLEFT, 0), (PRIGHT, 0), (LEFT, 1), (RIGHT, 1), (PLEFT, 1), (PRIGHT, 1)))
FIRST = ((RIGHT, 0), (PRIGHT, 0), (RIGHT, 1), (PRIGHT, 1), (LEFT, 0), (PLEFT, 0), (LEFT, 1), (PLEFT, 1))


def digits(order, which, base):
    return sum(step[which] * base ** n for n, step in enumerate(order))


def matern(minus_cross, own_sq, other_sq):
    x = jnp.maximum(minus_cross + own_sq + other_sq, 1e-30)
    u = x * lax.rsqrt(x)
    return jnp.exp2(SHIFT - u) * (u * (u + LIN) + CON)


def split(x, parts):
    out = []
    for _ in range(parts):
        piece = x.astype(jnp.bfloat16)
        out.append(piece)
        x = x - piece.astype(jnp.float32)
    return out


def kernel(n_lane, n_dev, p_hbm, v_hbm, scale_ref, o_ref,
           buf, norms, own_sq, left, acc, load_sem, send_sem, recv_sem, nsend_sem, nrecv_sem):
    pts = p_hbm.shape[0]
    n_piece = pts // PIECE
    me = lax.axis_index("blk") * n_lane + lax.axis_index("lane")
    core = lax.rem(me, 2)
    zero = 1 - (lax.rem(me // 2, RING) + RING - 1) // RING
    low = 1 - (lax.rem(me // 2, RING) + RING - 2) // RING

    def device(step):
        there = lax.rem(me + step + n_dev, n_dev)
        return (there // n_lane, lax.rem(there, n_lane))

    partner, outer = device(1 - 2 * core), device(2 * core - 1)
    lower, upper = device(-2), device(2)
    inputs = (p_hbm, v_hbm)

    barrier = pltpu.get_barrier_semaphore()
    for there in (partner, outer, lower, upper):
        pl.semaphore_signal(barrier, inc=1, device_id=there, device_id_type=MESH)
    loads = [pltpu.make_async_copy(inputs[k], buf.at[OWN, k], load_sem.at[k]) for k in range(2)]
    for load in loads:
        load.start()

    def copy(flow, src, dst, piece, there):
        rows = pl.ds(piece * PIECE, PIECE)
        return pltpu.make_async_remote_copy(
            buf.at[src, :, rows], buf.at[dst, :, rows], send_sem.at[flow, piece], recv_sem.at[dst, piece],
            device_id=there, device_id_type=MESH)

    def norm_copy(flow, src, dst, there):
        return pltpu.make_async_remote_copy(
            norms.at[src], norms.at[dst], nsend_sem.at[flow], nrecv_sem.at[dst],
            device_id=there, device_id_type=MESH)

    def send_own(piece):
        copy(0, OWN, RIGHT, piece, lower).start()
        copy(1, OWN, LEFT, piece, upper).start()
        copy(2, OWN, PARTNER, piece, partner).start()

    def arrived(slot, piece):
        copy(0, slot, slot, piece, partner).wait_recv()

    def prepare():
        gain = scale_ref[...] * (math.sqrt(5.0) * LOG2E)
        gain = gain * gain
        ones = jnp.ones((8, 384), jnp.bfloat16)
        for j in range(0, pts, 256):
            p = buf[OWN, 0, j:j + 256, :].astype(jnp.float32)
            hi, lo = split(-2.0 * (p * gain), 2)
            left[j:j + 256, 0:128] = hi
            left[j:j + 256, 128:256] = lo
            q = p * (-0.5 * (hi.astype(jnp.float32) + lo.astype(jnp.float32)))
            row = lax.dot_general(ones, jnp.concatenate(split(q, 3), axis=1), (((1,), (1,)), ((), ())),
                                  preferred_element_type=jnp.float32)
            own_sq[:, j:j + 256] = row
            norms[OWN, j // 128:j // 128 + 1, :] = row[0:1, 0:128]
            norms[OWN, j // 128 + 1:j // 128 + 2, :] = row[0:1, 128:256]
        acc[...] = jnp.zeros_like(acc)

    def compute(slot, j0, n_row):
        p = buf[slot, 0, pl.ds(j0, n_row), :]
        v = buf[slot, 1, pl.ds(j0, n_row), :]
        pp = jnp.concatenate([p, p], axis=1)
        vt = v.T
        v2 = jnp.concatenate([vt, vt], axis=1)
        cols = []
        for q in range(n_row // 128):
            row = norms[slot, pl.ds(j0 // 128 + q, 1), :]
            cols.append(jnp.broadcast_to(row, (128, 128)).T)
        other = jnp.concatenate(cols, axis=0)
        other = jnp.concatenate([other] * (COLS // 128), axis=1)
        for i in range(0, pts, COLS):
            c = lax.dot_general(pp, left[i:i + COLS, :], (((1,), (1,)), ((), ())),
                                preferred_element_type=jnp.float32)
            k = matern(c, own_sq[0:1, i:i + COLS], other)
            acc[:, i:i + COLS] += jnp.dot(v2, jnp.concatenate(split(k, 2), axis=0),
                                          preferred_element_type=jnp.float32)

    for load in loads:
        load.wait()
    n_half = pts // ROWS

    @pl.when(zero == 1)
    def _():
        prepare()
        lax.fori_loop(0, n_half, lambda half, c: (compute(OWN, half * ROWS, ROWS), c)[1], 0)

    pl.semaphore_wait(barrier, 4)
    send_own(0)

    @pl.when(zero == 0)
    def _():
        prepare()

    norm_copy(0, OWN, RIGHT, lower).start()
    norm_copy(1, OWN, LEFT, upper).start()
    norm_copy(2, OWN, PARTNER, partner).start()
    for piece in range(1, n_piece):
        send_own(piece)

    def near(half, _):
        @pl.when(half == n_half)
        def _():
            norm_copy(0, PARTNER, PARTNER, partner).wait_recv()
            for piece in range(n_piece):
                arrived(PARTNER, piece)

        compute(half // n_half, lax.rem(half, n_half) * ROWS, ROWS)
        return 0

    lax.fori_loop(zero * n_half, 2 * n_half, near, 0)

    passed_on = 3 - core
    early = low * core

    def far(n_row):
        norm_copy(0, FAR, FAR, partner).wait_recv()

        def part(n, _):
            for n_th in range(n_row // PIECE):
                arrived(FAR, n * (n_row // PIECE) + n_th)
            compute(FAR, n * n_row, n_row)
            return 0

        lax.fori_loop(0, pts // n_row, part, 0)

    def step(n, codes):
        slots, halves = codes
        slot, half = lax.rem(slots, 8), lax.rem(halves, 2)

        for near_slot in (LEFT, RIGHT):
            for piece in range(n_piece):
                when_low = 4 + piece // 2 if near_slot == LEFT else 2 * (piece // 2)
                when = low * when_low + (1 - low) * (0, 0, 1, 2)[piece]

                @pl.when(n == when)
                def _():
                    if piece == 0:
                        norm_copy(0, near_slot, near_slot, partner).wait_recv()
                        norm_copy(near_slot + 1, near_slot, near_slot + 2, partner).start()
                    arrived(near_slot, piece)

                    @pl.when(near_slot == passed_on)
                    def _():
                        if piece == 0:
                            norm_copy(5, near_slot, FAR, outer).start()
                        copy(5, near_slot, FAR, piece, outer).start()

                    copy(near_slot + 1, near_slot, near_slot + 2, piece, partner).start()

        @pl.when(n == 4 + 8 * (1 - early))
        def _():
            far(ROWS)

        @pl.when(slot >= PLEFT)
        def _():
            @pl.when(half == 0)
            def _():
                norm_copy(0, slot, slot, partner).wait_recv()

            for n_th in range(ROWS // PIECE):
                arrived(slot, half * (ROWS // PIECE) + n_th)

        compute(slot, half * ROWS, ROWS)
        return slots // 8, halves // 2

    slots = low * digits(FIRST, 0, 8) + (1 - low) * (
        (1 - core) * digits(INNER[0], 0, 8) + core * digits(INNER[1], 0, 8))
    halves = low * digits(FIRST, 1, 2) + (1 - low) * digits(INNER[0], 1, 2)
    lax.fori_loop(0, len(FIRST), step, (slots, halves))

    @pl.when(early == 0)
    def _():
        far(PIECE)

    for j in range(0, pts, 256):
        o_ref[j:j + 256, :] = acc[:, j:j + 256].T
    for flow in range(6):
        norm_copy(flow, OWN, PARTNER, partner).wait_send()
        for piece in range(n_piece):
            copy(flow, OWN, PARTNER, piece, partner).wait_send()


def body(n_lane, n_dev, points, probes, inv_scale, noise_var):
    pts, feats = points.shape
    n_piece = pts // PIECE
    product = pl.pallas_call(
        functools.partial(kernel, n_lane, n_dev),
        out_shape=jax.ShapeDtypeStruct((pts, feats), jnp.float32),
        in_specs=[pl.BlockSpec(memory_space=pl.ANY), pl.BlockSpec(memory_space=pl.ANY),
                  pl.BlockSpec(memory_space=pltpu.VMEM)],
        out_specs=pl.BlockSpec(memory_space=pltpu.VMEM),
        scratch_shapes=[
            pltpu.VMEM((7, 2, pts, feats), jnp.bfloat16),
            pltpu.VMEM((7, 8, 128), jnp.float32),
            pltpu.VMEM((8, pts), jnp.float32),
            pltpu.VMEM((pts, 2 * feats), jnp.bfloat16),
            pltpu.VMEM((feats, pts), jnp.float32),
            pltpu.SemaphoreType.DMA((2,)),
            pltpu.SemaphoreType.DMA((6, n_piece)),
            pltpu.SemaphoreType.DMA((7, n_piece)),
            pltpu.SemaphoreType.DMA((6,)),
            pltpu.SemaphoreType.DMA((7,)),
        ],
        compiler_params=pltpu.CompilerParams(collective_id=0, has_side_effects=True),
    )(points, probes, inv_scale.reshape(1, feats))
    return product + noise_var[0] * probes.astype(jnp.float32)


def solution(mesh):
    n_lane = mesh.shape["lane"]
    n_dev = n_lane * mesh.shape["blk"]
    in_specs = (P(("blk", "lane"), None), P(("blk", "lane"), None), P(), P())
    return jax.shard_map(functools.partial(body, n_lane, n_dev), mesh=mesh, in_specs=in_specs,
                         out_specs=P(("blk", "lane"), None), check_vma=False)
```

```python
import functools
import math

import jax
import jax.numpy as jnp
from jax import lax
from jax.experimental import pallas as pl
from jax.experimental.pallas import tpu as pltpu
from jax.sharding import PartitionSpec as P

MESH = pl.DeviceIdType.MESH
LOG2E = math.log2(math.e)
LN2 = math.log(2.0)
SHIFT = math.log2(LN2 * LN2 / 3.0)
LIN = 3.0 / LN2
CON = 3.0 / (LN2 * LN2)
PIECE = 256
ROWS = 512
COLS = 256
RING = 12

OWN, PARTNER, LEFT, RIGHT, PLEFT, PRIGHT, FAR = range(7)
INNER = (((RIGHT, 0), (LEFT, 0), (PRIGHT, 0), (PLEFT, 0), (RIGHT, 1), (LEFT, 1), (PRIGHT, 1), (PLEFT, 1)),
         ((LEFT, 0), (RIGHT, 0), (PLEFT, 0), (PRIGHT, 0), (LEFT, 1), (RIGHT, 1), (PLEFT, 1), (PRIGHT, 1)))
FIRST = ((RIGHT, 0), (PRIGHT, 0), (RIGHT, 1), (PRIGHT, 1), (LEFT, 0), (PLEFT, 0), (LEFT, 1), (PLEFT, 1))


def digits(order, which, base):
    return sum(step[which] * base ** n for n, step in enumerate(order))


def matern(minus_cross, own_sq, other_sq):
    x = jnp.maximum(minus_cross + own_sq + other_sq, 1e-30)
    u = x * lax.rsqrt(x)
    return jnp.exp2(SHIFT - u) * (u * (u + LIN) + CON)


def split(x, parts):
    out = []
    for _ in range(parts):
        piece = x.astype(jnp.bfloat16)
        out.append(piece)
        x = x - piece.astype(jnp.float32)
    return out


def kernel(n_lane, n_dev, p_hbm, v_hbm, scale_ref, o_ref,
           buf, norms, own_sq, left, acc, load_sem, send_sem, recv_sem, nsend_sem, nrecv_sem):
    pts = p_hbm.shape[0]
    n_piece = pts // PIECE
    me = lax.axis_index("blk") * n_lane + lax.axis_index("lane")
    core = lax.rem(me, 2)
    zero = 1 - (lax.rem(me // 2, RING) + RING - 1) // RING
    top = lax.rem(me // 2, RING) // (RING - 1)
    low = 1 - (lax.rem(me // 2, RING) + RING - 2) // RING

    def device(step):
        there = lax.rem(me + step + n_dev, n_dev)
        return (there // n_lane, lax.rem(there, n_lane))

    partner, outer = device(1 - 2 * core), device(2 * core - 1)
    lower, upper = device(-2), device(2)
    inputs = (p_hbm, v_hbm)

    barrier = pltpu.get_barrier_semaphore()

    def greet(*devices):
        for there in devices:
            pl.semaphore_signal(barrier, inc=1, device_id=there, device_id_type=MESH)

    greet(partner)

    @pl.when(zero == 0)
    def _():
        greet(lower)

    @pl.when(top == 0)
    def _():
        greet(upper)

    @pl.when(zero * (1 - core) + top * core == 0)
    def _():
        greet(outer)

    loads = [pltpu.make_async_copy(inputs[k], buf.at[OWN, k], load_sem.at[k]) for k in range(2)]
    for load in loads:
        load.start()

    def copy(flow, src, dst, piece, there):
        rows = pl.ds(piece * PIECE, PIECE)
        return pltpu.make_async_remote_copy(
            buf.at[src, :, rows], buf.at[dst, :, rows], send_sem.at[flow, piece], recv_sem.at[dst, piece],
            device_id=there, device_id_type=MESH)

    def norm_copy(flow, src, dst, there):
        return pltpu.make_async_remote_copy(
            norms.at[src], norms.at[dst], nsend_sem.at[flow], nrecv_sem.at[dst],
            device_id=there, device_id_type=MESH)

    def send_own(piece):
        @pl.when(zero == 0)
        def _():
            copy(0, OWN, RIGHT, piece, lower).start()

        copy(1, OWN, LEFT, piece, upper).start()
        copy(2, OWN, PARTNER, piece, partner).start()

    def arrived(slot, piece):
        copy(0, slot, slot, piece, partner).wait_recv()

    def prepare():
        gain = scale_ref[...] * (math.sqrt(5.0) * LOG2E)
        gain = gain * gain
        ones = jnp.ones((8, 384), jnp.bfloat16)
        for j in range(0, pts, 256):
            p = buf[OWN, 0, j:j + 256, :].astype(jnp.float32)
            hi, lo = split(-2.0 * (p * gain), 2)
            left[j:j + 256, 0:128] = hi
            left[j:j + 256, 128:256] = lo
            q = p * (-0.5 * (hi.astype(jnp.float32) + lo.astype(jnp.float32)))
            row = lax.dot_general(ones, jnp.concatenate(split(q, 3), axis=1), (((1,), (1,)), ((), ())),
                                  preferred_element_type=jnp.float32)
            own_sq[:, j:j + 256] = row
            norms[OWN, j // 128:j // 128 + 1, :] = row[0:1, 0:128]
            norms[OWN, j // 128 + 1:j // 128 + 2, :] = row[0:1, 128:256]
        acc[...] = jnp.zeros_like(acc)

    def compute(slot, j0, n_row):
        p = buf[slot, 0, pl.ds(j0, n_row), :]
        v = buf[slot, 1, pl.ds(j0, n_row), :]
        pp = jnp.concatenate([p, p], axis=1)
        vt = v.T
        v2 = jnp.concatenate([vt, vt], axis=1)
        cols = []
        for q in range(n_row // 128):
            row = norms[slot, pl.ds(j0 // 128 + q, 1), :]
            cols.append(jnp.broadcast_to(row, (128, 128)).T)
        other = jnp.concatenate(cols, axis=0)
        other = jnp.concatenate([other] * (COLS // 128), axis=1)
        for i in range(0, pts, COLS):
            c = lax.dot_general(pp, left[i:i + COLS, :], (((1,), (1,)), ((), ())),
                                preferred_element_type=jnp.float32)
            k = matern(c, own_sq[0:1, i:i + COLS], other)
            acc[:, i:i + COLS] += jnp.dot(v2, jnp.concatenate(split(k, 2), axis=0),
                                          preferred_element_type=jnp.float32)

    for load in loads:
        load.wait()
    n_half = pts // ROWS

    @pl.when(zero == 1)
    def _():
        prepare()
        lax.fori_loop(0, n_half, lambda half, c: (compute(OWN, half * ROWS, ROWS), c)[1], 0)

    pl.semaphore_wait(barrier, 4 - zero * (2 - core))

    @pl.when(zero + top == 1)
    def _():
        @pl.when(zero == 1)
        def _():
            greet(lower)

        @pl.when(top == 1)
        def _():
            greet(upper)

        @pl.when(zero * (1 - core) + top * core == 1)
        def _():
            greet(outer)

    send_own(0)

    @pl.when(zero == 0)
    def _():
        prepare()

    @pl.when(zero == 0)
    def _():
        norm_copy(0, OWN, RIGHT, lower).start()

    norm_copy(1, OWN, LEFT, upper).start()
    norm_copy(2, OWN, PARTNER, partner).start()
    for piece in range(1, n_piece):
        send_own(piece)

    def near(half, _):
        @pl.when(half == n_half)
        def _():
            norm_copy(0, PARTNER, PARTNER, partner).wait_recv()
            for piece in range(n_piece):
                arrived(PARTNER, piece)

        compute(half // n_half, lax.rem(half, n_half) * ROWS, ROWS)
        return 0

    lax.fori_loop(zero * n_half, 2 * n_half, near, 0)

    passed_on = 3 - core
    early = low * core

    def far(n_row):
        norm_copy(0, FAR, FAR, partner).wait_recv()

        def part(n, _):
            for n_th in range(n_row // PIECE):
                arrived(FAR, n * (n_row // PIECE) + n_th)
            compute(FAR, n * n_row, n_row)
            return 0

        lax.fori_loop(0, pts // n_row, part, 0)

    def step(n, codes):
        slots, halves = codes
        slot, half = lax.rem(slots, 8), lax.rem(halves, 2)

        @pl.when(n == 4 + 8 * (1 - early))
        def _():
            far(ROWS)

        @pl.when(n == 4 + 8 * (1 - zero))
        def _():
            pl.semaphore_wait(barrier, 2 - core)
            norm_copy(0, OWN, RIGHT, lower).start()
            for piece in range(n_piece):
                copy(0, OWN, RIGHT, piece, lower).start()

            @pl.when(core == 0)
            def _():
                norm_copy(5, RIGHT, FAR, outer).start()
                for piece in range(n_piece):
                    copy(5, RIGHT, FAR, piece, outer).start()

        for near_slot in (LEFT, RIGHT):
            for piece in range(n_piece):
                when_low = 4 + piece // 2 if near_slot == LEFT else 2 * (piece // 2)
                when = low * when_low + (1 - low) * (0, 0, 1, 2)[piece]

                @pl.when(n == when)
                def _():
                    if piece == 0:
                        norm_copy(0, near_slot, near_slot, partner).wait_recv()
                        norm_copy(near_slot + 1, near_slot, near_slot + 2, partner).start()
                    arrived(near_slot, piece)

                    @pl.when(near_slot + 8 * zero * (1 - core) == passed_on)
                    def _():
                        if piece == 0:
                            norm_copy(5, near_slot, FAR, outer).start()
                        copy(5, near_slot, FAR, piece, outer).start()

                    copy(near_slot + 1, near_slot, near_slot + 2, piece, partner).start()

        @pl.when(slot >= PLEFT)
        def _():
            @pl.when(half == 0)
            def _():
                norm_copy(0, slot, slot, partner).wait_recv()

            for n_th in range(ROWS // PIECE):
                arrived(slot, half * (ROWS // PIECE) + n_th)

        compute(slot, half * ROWS, ROWS)
        return slots // 8, halves // 2

    slots = low * digits(FIRST, 0, 8) + (1 - low) * (
        (1 - core) * digits(INNER[0], 0, 8) + core * digits(INNER[1], 0, 8))
    halves = low * digits(FIRST, 1, 2) + (1 - low) * digits(INNER[0], 1, 2)
    lax.fori_loop(0, len(FIRST), step, (slots, halves))

    @pl.when(early == 0)
    def _():
        far(PIECE)

    for j in range(0, pts, 256):
        o_ref[j:j + 256, :] = acc[:, j:j + 256].T
    for flow in range(6):
        norm_copy(flow, OWN, PARTNER, partner).wait_send()
        for piece in range(n_piece):
            copy(flow, OWN, PARTNER, piece, partner).wait_send()


def body(n_lane, n_dev, points, probes, inv_scale, noise_var):
    pts, feats = points.shape
    n_piece = pts // PIECE
    product = pl.pallas_call(
        functools.partial(kernel, n_lane, n_dev),
        out_shape=jax.ShapeDtypeStruct((pts, feats), jnp.float32),
        in_specs=[pl.BlockSpec(memory_space=pl.ANY), pl.BlockSpec(memory_space=pl.ANY),
                  pl.BlockSpec(memory_space=pltpu.VMEM)],
        out_specs=pl.BlockSpec(memory_space=pltpu.VMEM),
        scratch_shapes=[
            pltpu.VMEM((7, 2, pts, feats), jnp.bfloat16),
            pltpu.VMEM((7, 8, 128), jnp.float32),
            pltpu.VMEM((8, pts), jnp.float32),
            pltpu.VMEM((pts, 2 * feats), jnp.bfloat16),
            pltpu.VMEM((feats, pts), jnp.float32),
            pltpu.SemaphoreType.DMA((2,)),
            pltpu.SemaphoreType.DMA((6, n_piece)),
            pltpu.SemaphoreType.DMA((7, n_piece)),
            pltpu.SemaphoreType.DMA((6,)),
            pltpu.SemaphoreType.DMA((7,)),
        ],
        compiler_params=pltpu.CompilerParams(collective_id=0, has_side_effects=True),
    )(points, probes, inv_scale.reshape(1, feats))
    return product + noise_var[0] * probes.astype(jnp.float32)


def solution(mesh):
    n_lane = mesh.shape["lane"]
    n_dev = n_lane * mesh.shape["blk"]
    in_specs = (P(("blk", "lane"), None), P(("blk", "lane"), None), P(), P())
    return jax.shard_map(functools.partial(body, n_lane, n_dev), mesh=mesh, in_specs=in_specs,
                         out_specs=P(("blk", "lane"), None), check_vma=False)
```

```python
import functools
import math

import jax
import jax.numpy as jnp
from jax import lax
from jax.experimental import pallas as pl
from jax.experimental.pallas import tpu as pltpu
from jax.sharding import PartitionSpec as P

MESH = pl.DeviceIdType.MESH
LOG2E = math.log2(math.e)
LN2 = math.log(2.0)
SHIFT = math.log2(LN2 * LN2 / 3.0)
LIN = 3.0 / LN2
CON = 3.0 / (LN2 * LN2)
PIECE = 256
ROWS = 512
COLS = 256
RING = 12

OWN, PARTNER, LEFT, RIGHT, PLEFT, PRIGHT, FAR = range(7)
INNER = (((RIGHT, 0), (LEFT, 0), (PRIGHT, 0), (PLEFT, 0), (RIGHT, 1), (LEFT, 1), (PRIGHT, 1), (PLEFT, 1)),
         ((LEFT, 0), (RIGHT, 0), (PLEFT, 0), (PRIGHT, 0), (LEFT, 1), (RIGHT, 1), (PLEFT, 1), (PRIGHT, 1)))
FIRST = ((RIGHT, 0), (PRIGHT, 0), (RIGHT, 1), (PRIGHT, 1), (LEFT, 0), (PLEFT, 0), (LEFT, 1), (PLEFT, 1))

LAST = ((LEFT, 0), (PLEFT, 0), (LEFT, 1), (PLEFT, 1), (RIGHT, 0), (PRIGHT, 0), (RIGHT, 1), (PRIGHT, 1))


def digits(order, which, base):
    return sum(step[which] * base ** n for n, step in enumerate(order))


def matern(minus_cross, own_sq, other_sq):
    x = jnp.maximum(minus_cross + own_sq + other_sq, 1e-30)
    u = x * lax.rsqrt(x)
    return jnp.exp2(SHIFT - u) * (u * (u + LIN) + CON)


def split(x, parts):
    out = []
    for _ in range(parts):
        piece = x.astype(jnp.bfloat16)
        out.append(piece)
        x = x - piece.astype(jnp.float32)
    return out


def kernel(n_lane, n_dev, p_hbm, v_hbm, scale_ref, o_ref,
           buf, norms, own_sq, left, acc, load_sem, send_sem, recv_sem, nsend_sem, nrecv_sem):
    pts = p_hbm.shape[0]
    n_piece = pts // PIECE
    me = lax.axis_index("blk") * n_lane + lax.axis_index("lane")
    core = lax.rem(me, 2)
    zero = 1 - (lax.rem(me // 2, RING) + RING - 1) // RING
    top = lax.rem(me // 2, RING) // (RING - 1)
    low = 1 - (lax.rem(me // 2, RING) + RING - 2) // RING

    def device(step):
        there = lax.rem(me + step + n_dev, n_dev)
        return (there // n_lane, lax.rem(there, n_lane))

    partner, outer = device(1 - 2 * core), device(2 * core - 1)
    lower, upper = device(-2), device(2)
    inputs = (p_hbm, v_hbm)

    barrier = pltpu.get_barrier_semaphore()

    def greet(*devices):
        for there in devices:
            pl.semaphore_signal(barrier, inc=1, device_id=there, device_id_type=MESH)

    greet(partner)

    @pl.when(zero == 0)
    def _():
        greet(lower)

    @pl.when(top == 0)
    def _():
        greet(upper)

    @pl.when(zero * (1 - core) + top * core == 0)
    def _():
        greet(outer)

    loads = [pltpu.make_async_copy(inputs[k], buf.at[OWN, k], load_sem.at[k]) for k in range(2)]
    for load in loads:
        load.start()

    def copy(flow, src, dst, piece, there):
        rows = pl.ds(piece * PIECE, PIECE)
        return pltpu.make_async_remote_copy(
            buf.at[src, :, rows], buf.at[dst, :, rows], send_sem.at[flow, piece], recv_sem.at[dst, piece],
            device_id=there, device_id_type=MESH)

    def norm_copy(flow, src, dst, there):
        return pltpu.make_async_remote_copy(
            norms.at[src], norms.at[dst], nsend_sem.at[flow], nrecv_sem.at[dst],
            device_id=there, device_id_type=MESH)

    def send_own(piece):
        @pl.when(zero == 0)
        def _():
            copy(0, OWN, RIGHT, piece, lower).start()

        copy(1, OWN, LEFT, piece, upper).start()
        copy(2, OWN, PARTNER, piece, partner).start()

    def arrived(slot, piece):
        copy(0, slot, slot, piece, partner).wait_recv()

    def prepare():
        gain = scale_ref[...] * (math.sqrt(5.0) * LOG2E)
        gain = gain * gain
        ones = jnp.ones((8, 384), jnp.bfloat16)
        for j in range(0, pts, 256):
            p = buf[OWN, 0, j:j + 256, :].astype(jnp.float32)
            hi, lo = split(-2.0 * (p * gain), 2)
            left[j:j + 256, 0:128] = hi
            left[j:j + 256, 128:256] = lo
            q = p * (-0.5 * (hi.astype(jnp.float32) + lo.astype(jnp.float32)))
            row = lax.dot_general(ones, jnp.concatenate(split(q, 3), axis=1), (((1,), (1,)), ((), ())),
                                  preferred_element_type=jnp.float32)
            own_sq[:, j:j + 256] = row
            norms[OWN, j // 128:j // 128 + 1, :] = row[0:1, 0:128]
            norms[OWN, j // 128 + 1:j // 128 + 2, :] = row[0:1, 128:256]
        acc[...] = jnp.zeros_like(acc)

    def compute(slot, j0, n_row):
        p = buf[slot, 0, pl.ds(j0, n_row), :]
        v = buf[slot, 1, pl.ds(j0, n_row), :]
        pp = jnp.concatenate([p, p], axis=1)
        vt = v.T
        v2 = jnp.concatenate([vt, vt], axis=1)
        cols = []
        for q in range(n_row // 128):
            row = norms[slot, pl.ds(j0 // 128 + q, 1), :]
            cols.append(jnp.broadcast_to(row, (128, 128)).T)
        other = jnp.concatenate(cols, axis=0)
        other = jnp.concatenate([other] * (COLS // 128), axis=1)
        for i in range(0, pts, COLS):
            c = lax.dot_general(pp, left[i:i + COLS, :], (((1,), (1,)), ((), ())),
                                preferred_element_type=jnp.float32)
            k = matern(c, own_sq[0:1, i:i + COLS], other)
            acc[:, i:i + COLS] += jnp.dot(v2, jnp.concatenate(split(k, 2), axis=0),
                                          preferred_element_type=jnp.float32)

    for load in loads:
        load.wait()
    n_half = pts // ROWS

    pl.semaphore_wait(barrier, 4 - zero * (2 - core))

    @pl.when(zero + top == 1)
    def _():
        @pl.when(zero == 1)
        def _():
            greet(lower)

        @pl.when(top == 1)
        def _():
            greet(upper)

        @pl.when(zero * (1 - core) + top * core == 1)
        def _():
            greet(outer)

    send_own(0)

    prepare()

    @pl.when(zero == 0)
    def _():
        norm_copy(0, OWN, RIGHT, lower).start()

    norm_copy(1, OWN, LEFT, upper).start()
    norm_copy(2, OWN, PARTNER, partner).start()
    for piece in range(1, n_piece):
        send_own(piece)

    def near(half, _):
        @pl.when(half == n_half)
        def _():
            norm_copy(0, PARTNER, PARTNER, partner).wait_recv()
            for piece in range(n_piece):
                arrived(PARTNER, piece)

        compute(half // n_half, lax.rem(half, n_half) * ROWS, ROWS)
        return 0

    lax.fori_loop(0, 2 * n_half, near, 0)

    passed_on = 3 - core
    early = low * core

    def far(n_row):
        norm_copy(0, FAR, FAR, partner).wait_recv()

        def part(n, _):
            for n_th in range(n_row // PIECE):
                arrived(FAR, n * (n_row // PIECE) + n_th)
            compute(FAR, n * n_row, n_row)
            return 0

        lax.fori_loop(0, pts // n_row, part, 0)

    def step(n, codes):
        slots, halves = codes
        slot, half = lax.rem(slots, 8), lax.rem(halves, 2)

        @pl.when(n == 4 + 8 * (1 - early))
        def _():
            far(ROWS)

        @pl.when(n == 4 + 8 * (1 - zero))
        def _():
            pl.semaphore_wait(barrier, 2 - core)
            norm_copy(0, OWN, RIGHT, lower).start()
            for piece in range(n_piece):
                copy(0, OWN, RIGHT, piece, lower).start()

            @pl.when(core == 0)
            def _():
                norm_copy(5, RIGHT, FAR, outer).start()
                for piece in range(n_piece):
                    copy(5, RIGHT, FAR, piece, outer).start()

        for near_slot in (LEFT, RIGHT):
            for piece in range(n_piece):
                when_low = 4 + piece // 2 if near_slot == LEFT else 2 * (piece // 2)
                when_top = 4 + piece // 2 if near_slot == RIGHT else (0, 0, 1, 2)[piece]
                when = low * when_low + top * when_top + (1 - low - top) * (0, 0, 1, 2)[piece]

                @pl.when(n == when)
                def _():
                    if piece == 0:
                        norm_copy(0, near_slot, near_slot, partner).wait_recv()
                        norm_copy(near_slot + 1, near_slot, near_slot + 2, partner).start()
                    arrived(near_slot, piece)

                    @pl.when(near_slot + 8 * zero * (1 - core) == passed_on)
                    def _():
                        if piece == 0:
                            norm_copy(5, near_slot, FAR, outer).start()
                        copy(5, near_slot, FAR, piece, outer).start()

                    copy(near_slot + 1, near_slot, near_slot + 2, piece, partner).start()

        @pl.when(slot >= PLEFT)
        def _():
            @pl.when(half == 0)
            def _():
                norm_copy(0, slot, slot, partner).wait_recv()

            for n_th in range(ROWS // PIECE):
                arrived(slot, half * (ROWS // PIECE) + n_th)

        compute(slot, half * ROWS, ROWS)
        return slots // 8, halves // 2

    slots = low * digits(FIRST, 0, 8) + top * digits(LAST, 0, 8) + (1 - low - top) * (
        (1 - core) * digits(INNER[0], 0, 8) + core * digits(INNER[1], 0, 8))
    halves = (low + top) * digits(FIRST, 1, 2) + (1 - low - top) * digits(INNER[0], 1, 2)
    lax.fori_loop(0, len(FIRST), step, (slots, halves))

    @pl.when(early == 0)
    def _():
        far(PIECE)

    for j in range(0, pts, 256):
        o_ref[j:j + 256, :] = acc[:, j:j + 256].T
    for flow in range(6):
        norm_copy(flow, OWN, PARTNER, partner).wait_send()
        for piece in range(n_piece):
            copy(flow, OWN, PARTNER, piece, partner).wait_send()


def body(n_lane, n_dev, points, probes, inv_scale, noise_var):
    pts, feats = points.shape
    n_piece = pts // PIECE
    product = pl.pallas_call(
        functools.partial(kernel, n_lane, n_dev),
        out_shape=jax.ShapeDtypeStruct((pts, feats), jnp.float32),
        in_specs=[pl.BlockSpec(memory_space=pl.ANY), pl.BlockSpec(memory_space=pl.ANY),
                  pl.BlockSpec(memory_space=pltpu.VMEM)],
        out_specs=pl.BlockSpec(memory_space=pltpu.VMEM),
        scratch_shapes=[
            pltpu.VMEM((7, 2, pts, feats), jnp.bfloat16),
            pltpu.VMEM((7, 8, 128), jnp.float32),
            pltpu.VMEM((8, pts), jnp.float32),
            pltpu.VMEM((pts, 2 * feats), jnp.bfloat16),
            pltpu.VMEM((feats, pts), jnp.float32),
            pltpu.SemaphoreType.DMA((2,)),
            pltpu.SemaphoreType.DMA((6, n_piece)),
            pltpu.SemaphoreType.DMA((7, n_piece)),
            pltpu.SemaphoreType.DMA((6,)),
            pltpu.SemaphoreType.DMA((7,)),
        ],
        compiler_params=pltpu.CompilerParams(collective_id=0, has_side_effects=True),
    )(points, probes, inv_scale.reshape(1, feats))
    return product + noise_var[0] * probes.astype(jnp.float32)


def solution(mesh):
    n_lane = mesh.shape["lane"]
    n_dev = n_lane * mesh.shape["blk"]
    in_specs = (P(("blk", "lane"), None), P(("blk", "lane"), None), P(), P())
    return jax.shard_map(functools.partial(body, n_lane, n_dev), mesh=mesh, in_specs=in_specs,
                         out_specs=P(("blk", "lane"), None), check_vma=False)
```

```python
import functools
import math

import jax
import jax.numpy as jnp
from jax import lax
from jax.experimental import pallas as pl
from jax.experimental.pallas import tpu as pltpu
from jax.sharding import PartitionSpec as P

MESH = pl.DeviceIdType.MESH
LOG2E = math.log2(math.e)
LN2 = math.log(2.0)
SHIFT = math.log2(LN2 * LN2 / 3.0)
LIN = 3.0 / LN2
CON = 3.0 / (LN2 * LN2)
PIECE = 256
ROWS = 512
COLS = 256
RING = 12

OWN, PARTNER, LEFT, RIGHT, PLEFT, PRIGHT, FAR = range(7)
INNER = (((RIGHT, 0), (LEFT, 0), (PRIGHT, 0), (PLEFT, 0), (RIGHT, 1), (LEFT, 1), (PRIGHT, 1), (PLEFT, 1)),
         ((LEFT, 0), (RIGHT, 0), (PLEFT, 0), (PRIGHT, 0), (LEFT, 1), (RIGHT, 1), (PLEFT, 1), (PRIGHT, 1)))
FIRST = ((RIGHT, 0), (PRIGHT, 0), (RIGHT, 1), (PRIGHT, 1), (LEFT, 0), (PLEFT, 0), (LEFT, 1), (PLEFT, 1))


def digits(order, which, base):
    return sum(step[which] * base ** n for n, step in enumerate(order))


def matern(minus_cross, own_sq, other_sq):
    x = jnp.maximum(minus_cross + own_sq + other_sq, 1e-30)
    u = x * lax.rsqrt(x)
    return jnp.exp2(SHIFT - u) * (u * (u + LIN) + CON)


def split(x, parts):
    out = []
    for _ in range(parts):
        piece = x.astype(jnp.bfloat16)
        out.append(piece)
        x = x - piece.astype(jnp.float32)
    return out


def kernel(n_lane, n_dev, p_hbm, v_hbm, scale_ref, o_ref,
           buf, norms, own_sq, left, acc, load_sem, send_sem, recv_sem, nsend_sem, nrecv_sem):
    pts = p_hbm.shape[0]
    n_piece = pts // PIECE
    me = lax.axis_index("blk") * n_lane + lax.axis_index("lane")
    core = lax.rem(me, 2)
    zero = 1 - (lax.rem(me // 2, RING) + RING - 1) // RING
    low = 1 - (lax.rem(me // 2, RING) + RING - 2) // RING

    def device(step):
        there = lax.rem(me + step + n_dev, n_dev)
        return (there // n_lane, lax.rem(there, n_lane))

    partner, outer = device(1 - 2 * core), device(2 * core - 1)
    lower, upper = device(-2), device(2)
    inputs = (p_hbm, v_hbm)

    barrier = pltpu.get_barrier_semaphore()
    for there in (partner, outer, lower, upper):
        pl.semaphore_signal(barrier, inc=1, device_id=there, device_id_type=MESH)
    loads = [pltpu.make_async_copy(inputs[k], buf.at[OWN, k], load_sem.at[k]) for k in range(2)]
    for load in loads:
        load.start()

    def copy(flow, src, dst, piece, there):
        rows = pl.ds(piece * PIECE, PIECE)
        return pltpu.make_async_remote_copy(
            buf.at[src, :, rows], buf.at[dst, :, rows], send_sem.at[flow, piece], recv_sem.at[dst, piece],
            device_id=there, device_id_type=MESH)

    def norm_copy(flow, src, dst, there):
        return pltpu.make_async_remote_copy(
            norms.at[src], norms.at[dst], nsend_sem.at[flow], nrecv_sem.at[dst],
            device_id=there, device_id_type=MESH)

    def send_own(piece):
        copy(0, OWN, RIGHT, piece, lower).start()
        copy(1, OWN, LEFT, piece, upper).start()
        copy(2, OWN, PARTNER, piece, partner).start()

    def arrived(slot, piece):
        copy(0, slot, slot, piece, partner).wait_recv()

    def prepare():
        gain = scale_ref[...] * (math.sqrt(5.0) * LOG2E)
        gain = gain * gain
        ones = jnp.ones((8, 384), jnp.bfloat16)
        for j in range(0, pts, 256):
            p = buf[OWN, 0, j:j + 256, :].astype(jnp.float32)
            hi, lo = split(-2.0 * (p * gain), 2)
            left[j:j + 256, 0:128] = hi
            left[j:j + 256, 128:256] = lo
            q = p * (-0.5 * (hi.astype(jnp.float32) + lo.astype(jnp.float32)))
            row = lax.dot_general(ones, jnp.concatenate(split(q, 3), axis=1), (((1,), (1,)), ((), ())),
                                  preferred_element_type=jnp.float32)
            own_sq[:, j:j + 256] = row
            norms[OWN, j // 128:j // 128 + 1, :] = row[0:1, 0:128]
            norms[OWN, j // 128 + 1:j // 128 + 2, :] = row[0:1, 128:256]
        acc[...] = jnp.zeros_like(acc)

    def compute(slot, j0, n_row):
        p = buf[slot, 0, pl.ds(j0, n_row), :]
        v = buf[slot, 1, pl.ds(j0, n_row), :]
        pp = jnp.concatenate([p, p], axis=1)
        vt = v.T
        v2 = jnp.concatenate([vt, vt], axis=1)
        cols = []
        for q in range(n_row // 128):
            row = norms[slot, pl.ds(j0 // 128 + q, 1), :]
            cols.append(jnp.broadcast_to(row, (128, 128)).T)
        other = jnp.concatenate(cols, axis=0)
        other = jnp.concatenate([other] * (COLS // 128), axis=1)
        for i in range(0, pts, COLS):
            c = lax.dot_general(pp, left[i:i + COLS, :], (((1,), (1,)), ((), ())),
                                preferred_element_type=jnp.float32)
            k = matern(c, own_sq[0:1, i:i + COLS], other)
            acc[:, i:i + COLS] += jnp.dot(v2, jnp.concatenate(split(k, 2), axis=0),
                                          preferred_element_type=jnp.float32)

    for load in loads:
        load.wait()
    n_half = pts // ROWS

    @pl.when(zero == 1)
    def _():
        prepare()
        lax.fori_loop(0, n_half, lambda half, c: (compute(OWN, half * ROWS, ROWS), c)[1], 0)

    pl.semaphore_wait(barrier, 4)
    send_own(0)

    @pl.when(zero == 0)
    def _():
        prepare()

    norm_copy(0, OWN, RIGHT, lower).start()
    norm_copy(1, OWN, LEFT, upper).start()
    norm_copy(2, OWN, PARTNER, partner).start()
    for piece in range(1, n_piece):
        send_own(piece)

    def near(half, _):
        @pl.when(half == n_half)
        def _():
            norm_copy(0, PARTNER, PARTNER, partner).wait_recv()
            for piece in range(n_piece):
                arrived(PARTNER, piece)

        compute(half // n_half, lax.rem(half, n_half) * ROWS, ROWS)
        return 0

    lax.fori_loop(zero * n_half, 2 * n_half, near, 0)

    passed_on = 3 - core
    early = low * core

    def far(n_row):
        norm_copy(0, FAR, FAR, partner).wait_recv()

        def part(n, _):
            for n_th in range(n_row // PIECE):
                arrived(FAR, n * (n_row // PIECE) + n_th)
            compute(FAR, n * n_row, n_row)
            return 0

        lax.fori_loop(0, pts // n_row, part, 0)

    def step(n, codes):
        slots, halves = codes
        slot, half = lax.rem(slots, 8), lax.rem(halves, 2)

        for near_slot in (LEFT, RIGHT):
            for piece in range(n_piece):
                when_low = 4 + piece // 2 if near_slot == LEFT else 2 * (piece // 2)
                when = low * when_low + (1 - low) * (0, 0, 1, 2)[piece]

                @pl.when(n == when)
                def _():
                    if piece == 0:
                        norm_copy(0, near_slot, near_slot, partner).wait_recv()
                        norm_copy(near_slot + 1, near_slot, near_slot + 2, partner).start()
                    arrived(near_slot, piece)

                    @pl.when(near_slot == passed_on)
                    def _():
                        if piece == 0:
                            norm_copy(5, near_slot, FAR, outer).start()
                        copy(5, near_slot, FAR, piece, outer).start()

                    copy(near_slot + 1, near_slot, near_slot + 2, piece, partner).start()

        @pl.when(n == 4 + 8 * (1 - early))
        def _():
            far(ROWS)

        @pl.when(slot >= PLEFT)
        def _():
            @pl.when(half == 0)
            def _():
                norm_copy(0, slot, slot, partner).wait_recv()

            @pl.when(n + early < 8)
            def _():
                for n_th in range(ROWS // PIECE):
                    arrived(slot, half * (ROWS // PIECE) + n_th)

        @pl.when(n + early < 8)
        def _():
            compute(slot, half * ROWS, ROWS)

        @pl.when(n + early == 8)
        def _():
            def part(n_th, _):
                arrived(slot, half * (ROWS // PIECE) + n_th)
                compute(slot, half * ROWS + n_th * PIECE, PIECE)
                return 0

            lax.fori_loop(0, ROWS // PIECE, part, 0)

        return slots // 8, halves // 2

    slots = low * digits(FIRST, 0, 8) + (1 - low) * (
        (1 - core) * digits(INNER[0], 0, 8) + core * digits(INNER[1], 0, 8))
    halves = low * digits(FIRST, 1, 2) + (1 - low) * digits(INNER[0], 1, 2)
    lax.fori_loop(0, len(FIRST), step, (slots, halves))

    @pl.when(early == 0)
    def _():
        far(PIECE)

    for j in range(0, pts, 256):
        o_ref[j:j + 256, :] = acc[:, j:j + 256].T
    for flow in range(6):
        norm_copy(flow, OWN, PARTNER, partner).wait_send()
        for piece in range(n_piece):
            copy(flow, OWN, PARTNER, piece, partner).wait_send()


def body(n_lane, n_dev, points, probes, inv_scale, noise_var):
    pts, feats = points.shape
    n_piece = pts // PIECE
    product = pl.pallas_call(
        functools.partial(kernel, n_lane, n_dev),
        out_shape=jax.ShapeDtypeStruct((pts, feats), jnp.float32),
        in_specs=[pl.BlockSpec(memory_space=pl.ANY), pl.BlockSpec(memory_space=pl.ANY),
                  pl.BlockSpec(memory_space=pltpu.VMEM)],
        out_specs=pl.BlockSpec(memory_space=pltpu.VMEM),
        scratch_shapes=[
            pltpu.VMEM((7, 2, pts, feats), jnp.bfloat16),
            pltpu.VMEM((7, 8, 128), jnp.float32),
            pltpu.VMEM((8, pts), jnp.float32),
            pltpu.VMEM((pts, 2 * feats), jnp.bfloat16),
            pltpu.VMEM((feats, pts), jnp.float32),
            pltpu.SemaphoreType.DMA((2,)),
            pltpu.SemaphoreType.DMA((6, n_piece)),
            pltpu.SemaphoreType.DMA((7, n_piece)),
            pltpu.SemaphoreType.DMA((6,)),
            pltpu.SemaphoreType.DMA((7,)),
        ],
        compiler_params=pltpu.CompilerParams(collective_id=0, has_side_effects=True),
    )(points, probes, inv_scale.reshape(1, feats))
    return product + noise_var[0] * probes.astype(jnp.float32)


def solution(mesh):
    n_lane = mesh.shape["lane"]
    n_dev = n_lane * mesh.shape["blk"]
    in_specs = (P(("blk", "lane"), None), P(("blk", "lane"), None), P(), P())
    return jax.shard_map(functools.partial(body, n_lane, n_dev), mesh=mesh, in_specs=in_specs,
                         out_specs=P(("blk", "lane"), None), check_vma=False)
```
